512 devices in a mesh: section: 4 (over x), strip: 128 (over z, y, core).
Axes of the slice: x: 4, y: 8, z: 8, core: 2. Of those that a mesh axis runs over, the one named last changes fastest.
Arguments:
- cotangent: bfloat16 [1, 8192, 2048], P(None, 'strip'), may hold values from -6 to 6
- activations: bfloat16 [4, 1, 8192, 2048], P('section', None, 'strip'), may hold values from -6 to 6
- weights: bfloat16 [4, 2, 3, 3, 64, 64], P('section'), may hold values from -0.25 to 0.25
- biases: float32 [4, 2, 64], P('section'), may hold values from -3 to 3
Outputs:
- noise_grad: bfloat16 [4, 1, 8192, 2048], P('section', None, 'strip')
- weight_grad: float32 [4, 2, 3, 3, 64, 64], P('section')
- bias_grad: float32 [4, 2, 64], P('section')
The draws below stay inside these ranges and needn't reach their ends.
All inputs are finite; a program needn't handle non-finite values.
Results may differ from the reference program's by a relative error of at most 0.01.
Values may be sent and summed in bfloat16 or wider, within the bound.
A program may use at most 64 MiB of HBM per device.

```python
import math
import jax
import jax.numpy as jnp
from jax import lax

CH = 64
CONVS = 2
ROWS = 64
COLS = 32
SAMPLES = 1
SECTIONS = 4
HEIGHT = 8192
N_STRIP = 128


def level_of(stream_key, dims, shards, least, top_value):
    def one(axis_at, parts):
        steps = jax.random.uniform(jax.random.fold_in(jax.random.fold_in(stream_key, 6), axis_at), (parts,), jnp.float32, least / len(shards), top_value / len(shards))
        return jnp.repeat(jnp.exp(steps), dims[axis_at] // parts).reshape((-1,) + (1,) * (len(dims) - axis_at - 1))

    level = one(*shards[0])
    for cut in shards[1:]:
        level = level * one(*cut)
    return level


def gaussian(rng, shape, deviation, reach, cuts=(), kind=jnp.bfloat16):
    result = jax.random.normal(rng, shape, jnp.float32) * deviation
    if len(cuts) > 0:
        result = level_of(rng, shape, cuts, -0.22, 0.18) * result
    return jnp.clip(result, min=-reach, max=reach).astype(kind)


def setup_inputs(seed: int = 0) -> dict:
    arg_keys = jax.random.split(jax.random.key(seed), 5)
    cotangent = gaussian(arg_keys[0], (SAMPLES, HEIGHT, COLS * CH), 1.0, 6.0, ((1, 128),))
    activations = gaussian(arg_keys[1], (SECTIONS, SAMPLES, HEIGHT, COLS * CH), 1.0, 6.0, ((0, 4), (2, 128)))
    weights = gaussian(arg_keys[2], (SECTIONS, CONVS, 3, 3, CH, CH), (9 * CH) ** -0.5, 0.25, ((0, 4),))
    biases = gaussian(arg_keys[3], (SECTIONS, CONVS, CH), 0.5, 3.0, ((0, 4),), jnp.float32)
    return dict(cotangent=cotangent, activations=activations, weights=weights, biases=biases)


LEAK = 0.05

def activate(value):
    return LEAK * value + (1.0 - LEAK) * jax.nn.softplus(value)

def steepness(value):
    return LEAK + (1.0 - LEAK) * jax.nn.sigmoid(value)

def conv_same(field_in, kernel):
    return lax.conv_general_dilated(field_in, kernel, (1, 1), ((1, 1), (1, 1)), dimension_numbers=('NHWC', 'HWIO', 'NHWC'), preferred_element_type=jnp.float32)

def flipped(kernel):
    return jnp.transpose(kernel[::-1, ::-1], (0, 1, 3, 2))

def weight_taps(field_in, error):
    padded = jnp.pad(field_in, ((0, 0), (1, 1), (1, 1), (0, 0)))
    height = error.shape[1]
    col_span = error.shape[2]
    tap_list = []
    for row_tap in range(3):
        for col_tap in range(3):
            window = padded[:, row_tap:row_tap + height, col_tap:col_tap + col_span].reshape(-1, CH)
            tap_list.append(jnp.dot(window.T, error.reshape(-1, CH), preferred_element_type=jnp.float32))
    return jnp.stack(tap_list).reshape(3, 3, CH, CH)

def coarsen(grad_up, section_level):
    fine_rows = ROWS * 3 ** section_level // 4 ** section_level
    coarse_rows = ROWS * 3 ** (section_level + 1) // 4 ** (section_level + 1)
    fine_cols = COLS * 3 ** section_level // 4 ** section_level
    coarse_cols = COLS * 3 ** (section_level + 1) // 4 ** (section_level + 1)
    fine_height = N_STRIP * fine_rows
    coarse_height = N_STRIP * coarse_rows
    wide_grad = grad_up.astype(jnp.float32)
    row_pos = jnp.arange(fine_height, dtype=jnp.int32)
    row_num = jnp.maximum(6 * row_pos - 1, 0)
    row_low = row_num // 8
    row_frac = (row_num - 8 * row_low).astype(jnp.float32) / 8.0
    row_high = jnp.minimum(row_low + 1, coarse_height - 1)
    by_rows = jnp.zeros((SAMPLES, coarse_height, fine_cols, CH), jnp.float32)
    by_rows = by_rows.at[:, row_low].add(wide_grad * (1.0 - row_frac)[None, :, None, None])
    by_rows = by_rows.at[:, row_high].add(wide_grad * row_frac[None, :, None, None])
    col_pos = jnp.arange(fine_cols, dtype=jnp.int32)
    col_num = jnp.maximum((2 * col_pos + 1) * coarse_cols - fine_cols, 0)
    col_den = 2 * fine_cols
    col_low = col_num // col_den
    col_frac = (col_num - col_den * col_low).astype(jnp.float32) / float(col_den)
    col_high = jnp.minimum(col_low + 1, coarse_cols - 1)
    by_cols = jnp.zeros((SAMPLES, coarse_height, coarse_cols, CH), jnp.float32)
    by_cols = by_cols.at[:, :, col_low].add(by_rows * (1.0 - col_frac)[None, None, :, None])
    by_cols = by_cols.at[:, :, col_high].add(by_rows * col_frac[None, None, :, None])
    return by_cols.astype(jnp.bfloat16)

def reference(cotangent, activations, weights, biases):
    grad_out = cotangent.reshape(SAMPLES, HEIGHT, COLS, CH)
    noise_list = []
    kernel_list = []
    bias_list = []
    for section_level in range(SECTIONS):
        live_rows = ROWS * 3 ** section_level // 4 ** section_level
        live_cols = COLS * 3 ** section_level // 4 ** section_level
        field_in = activations[section_level].reshape(SAMPLES, N_STRIP, ROWS, COLS, CH)[:, :, :live_rows, :live_cols]
        field_in = field_in.reshape(SAMPLES, N_STRIP * live_rows, live_cols, CH)
        kernel_in = weights[section_level, 0]
        kernel_out = weights[section_level, 1]
        pre_in = conv_same(field_in, kernel_in) + biases[section_level, 0]
        hidden = activate(pre_in).astype(jnp.bfloat16)
        pre_out = conv_same(hidden, kernel_out) + biases[section_level, 1]
        error_out = (grad_out.astype(jnp.float32) * steepness(pre_out)).astype(jnp.bfloat16)
        back_hidden = conv_same(error_out, flipped(kernel_out))
        error_in = (back_hidden * steepness(pre_in)).astype(jnp.bfloat16)
        back_input = conv_same(error_in, flipped(kernel_in))
        grad_up = (grad_out.astype(jnp.float32) + back_input).astype(jnp.bfloat16)
        scale_back = 1.0 / math.sqrt(SAMPLES * N_STRIP * live_rows * live_cols)
        kernel_list.append(jnp.stack([weight_taps(field_in, error_in), weight_taps(hidden, error_out)]) * scale_back)
        bias_list.append(jnp.stack([lax.optimization_barrier(jnp.sum(error_in.astype(jnp.float32), axis=(0, 1, 2))), lax.optimization_barrier(jnp.sum(error_out.astype(jnp.float32), axis=(0, 1, 2)))]) * scale_back)
        noise = back_input.astype(jnp.bfloat16).reshape(SAMPLES, N_STRIP, live_rows, live_cols, CH)
        noise = jnp.pad(noise, ((0, 0), (0, 0), (0, ROWS - live_rows), (0, COLS - live_cols), (0, 0)))
        noise_list.append(noise.reshape(SAMPLES, HEIGHT, COLS * CH))
        if section_level + 1 < SECTIONS:
            grad_out = coarsen(grad_up, section_level)
    return (jnp.stack(noise_list), jnp.stack(kernel_list), jnp.stack(bias_list))
```

```python
import jax
import jax.numpy as jnp
from jax import lax
from jax.experimental import pallas as pl
from jax.experimental.pallas import tpu as pltpu
from jax.sharding import PartitionSpec as P

LEAK = 0.05


def extended_2(cells, sides, width):
    for axis, dim in sides:
        count = lax.axis_size(axis)
        ends = count - 1
        head = lax.slice_in_dim(cells, 0, width, axis=dim)
        tail = lax.slice_in_dim(cells, cells.shape[dim] - width, cells.shape[dim], axis=dim)
        cells = jnp.concatenate(
            [
                lax.ppermute(tail, axis, [(i, (i + 1) % count) for i in range(ends)]),
                cells,
                lax.ppermute(head, axis, [((i + 1) % count, i) for i in range(ends)]),
            ],
            axis=dim,
        )
    return cells


def shifted_2(x, axis, by):
    peers = lax.axis_size(axis)
    pairs = [(i, i + by) for i in range(peers) if 0 <= i + by < peers]
    return lax.ppermute(x, axis, pairs)


def activate(value):
    return LEAK * value + (1.0 - LEAK) * jax.nn.softplus(value)


def steepness(value):
    return LEAK + (1.0 - LEAK) * jax.nn.sigmoid(value)


def conv_rows(field_in, kernel):
    return lax.conv_general_dilated(
        field_in,
        kernel,
        (1, 1),
        ((0, 0), (1, 1)),
        dimension_numbers=("NHWC", "HWIO", "NHWC"),
        preferred_element_type=jnp.float32,
    )


def flipped(kernel):
    return jnp.transpose(kernel[::-1, ::-1], (0, 1, 3, 2))


def weight_taps(extended, error):
    padded = jnp.pad(extended, ((0, 0), (0, 0), (1, 1), (0, 0)))
    height = error.shape[1]
    col_span = error.shape[2]
    channels = error.shape[3]
    tap_list = []
    for row_tap in range(3):
        for col_tap in range(3):
            window = padded[:, row_tap : row_tap + height, col_tap : col_tap + col_span]
            tap_list.append(
                lax.dot_general(
                    window,
                    error,
                    (((0, 1, 2), (0, 1, 2)), ((), ())),
                    preferred_element_type=jnp.float32,
                )
            )
    return jnp.stack(tap_list).reshape(3, 3, channels, channels)


def edge_rows(field_in, rim_depth, live_rows):
    upper_rows = field_in[:, :rim_depth]
    lower_rows = lax.dynamic_slice_in_dim(field_in, live_rows - rim_depth, rim_depth, 1)
    return jnp.concatenate([upper_rows, lower_rows], axis=1)


def attach(field_in, received, rim_depth, live_rows):
    upper_rows = received[:, :rim_depth]
    lower_rows = received[:, 3 * rim_depth :]
    filler = jnp.zeros_like(upper_rows)
    joined = jnp.concatenate([upper_rows, field_in, filler], axis=1)
    return lax.dynamic_update_slice_in_dim(joined, lower_rows, live_rows + rim_depth, 1)


RING = 8
PIECE = 40
HALF = RING * PIECE
PACKED = 2 * HALF
MESH = pl.DeviceIdType.MESH


def reduce_body(
    src, out, pair_in, y_sum, y_in, z_out, z_in, gathered,
    pair_send, pair_recv, y_send, y_recv, z_send, z_recv, g_send, g_recv, p_send, p_recv,
):
    strip = lax.axis_index("strip")
    core = lax.rem(strip, 2)
    row = lax.rem(lax.div(strip, 2), RING)
    deep = lax.div(strip, 2 * RING)
    partner = strip + 1 - 2 * core

    def y_peer(step):
        return (deep * RING + lax.rem(row + step, RING)) * 2 + core

    def z_peer(step):
        return (lax.rem(deep + step, RING) * RING + row) * 2 + core

    def remote(src_ref, dst_ref, send, recv, strip_id):
        return pltpu.make_async_remote_copy(
            src_ref=src_ref,
            dst_ref=dst_ref,
            send_sem=send,
            recv_sem=recv,
            device_id=(lax.axis_index("section"), strip_id),
            device_id_type=MESH,
        )

    barrier = pltpu.get_barrier_semaphore()
    peers = [partner]
    peers += [y_peer(step) for step in range(1, RING)]
    peers += [z_peer(step) for step in range(1, RING)]
    for peer in peers:
        pl.semaphore_signal(
            barrier,
            inc=1,
            device_id=(lax.axis_index("section"), peer),
            device_id_type=MESH,
        )
    pl.semaphore_wait(barrier, len(peers))

    mine = pl.multiple_of(core * HALF, 8)
    other = pl.multiple_of((1 - core) * HALF, 8)
    swap = remote(src.at[pl.ds(other, HALF)], pair_in, pair_send, pair_recv, partner)
    swap.start()
    swap.wait()
    y_sum[...] = src[pl.ds(mine, HALF), :] + pair_in[...]

    def piece(ref, index):
        return ref.at[pl.ds(pl.multiple_of(index * PIECE, 8), PIECE)]

    scatter = []
    for step in range(1, RING):
        copy = remote(
            piece(y_sum, lax.rem(row + step, RING)),
            y_in.at[step - 1],
            y_send.at[step - 1],
            y_recv.at[step - 1],
            y_peer(step),
        )
        copy.start()
        scatter.append(copy)
    total = y_sum[pl.ds(pl.multiple_of(row * PIECE, 8), PIECE), :]
    for step in range(1, RING):
        scatter[step - 1].wait_recv()
        total = total + y_in[step - 1]
    z_out[...] = total
    z_in[deep] = total
    trade = []
    for step in range(1, RING):
        copy = remote(
            z_out, z_in.at[deep], z_send.at[step - 1], z_recv.at[step - 1], z_peer(step)
        )
        copy.start()
        trade.append(copy)
    for copy in trade:
        copy.wait_recv()
    total = z_in[0]
    for index in range(1, RING):
        total = total + z_in[index]
    own = core * RING + row
    gathered[pl.ds(pl.multiple_of(own * PIECE, 8), PIECE), :] = total
    gather = []
    for step in range(1, RING):
        copy = remote(
            piece(gathered, own),
            piece(gathered, own),
            g_send.at[step - 1],
            g_recv.at[step - 1],
            y_peer(step),
        )
        copy.start()
        gather.append(copy)
    passed = []
    copy = remote(piece(gathered, own), piece(gathered, own), p_send.at[0], p_recv.at[0], partner)
    copy.start()
    passed.append(copy)
    for step in range(1, RING):
        gather[step - 1].wait_recv()
        came = core * RING + lax.rem(row + RING - step, RING)
        copy = remote(
            piece(gathered, came),
            piece(gathered, came),
            p_send.at[step],
            p_recv.at[step],
            partner,
        )
        copy.start()
        passed.append(copy)
    for copy in passed:
        copy.wait_recv()
    out[...] = gathered[...]
    for copy in scatter + trade + gather + passed:
        copy.wait_send()


def strip_sum(packed):
    dma = pltpu.SemaphoreType.DMA
    return pl.pallas_call(
        reduce_body,
        out_shape=jax.ShapeDtypeStruct((PACKED, 128), jnp.float32),
        in_specs=[pl.BlockSpec(memory_space=pltpu.VMEM)],
        out_specs=pl.BlockSpec(memory_space=pltpu.VMEM),
        scratch_shapes=[
            pltpu.VMEM((HALF, 128), jnp.float32),
            pltpu.VMEM((HALF, 128), jnp.float32),
            pltpu.VMEM((RING - 1, PIECE, 128), jnp.float32),
            pltpu.VMEM((PIECE, 128), jnp.float32),
            pltpu.VMEM((RING, PIECE, 128), jnp.float32),
            pltpu.VMEM((PACKED, 128), jnp.float32),
            dma, dma,
            dma((RING - 1,)), dma((RING - 1,)),
            dma((RING - 1,)), dma((RING - 1,)),
            dma((RING - 1,)), dma((RING - 1,)),
            dma((RING,)), dma((RING,)),
        ],
        compiler_params=pltpu.CompilerParams(collective_id=1, has_side_effects=True),
    )(packed)


def local(cotangent, activations, weights, biases):
    section_id = lax.axis_index("section")
    strip_id = lax.axis_index("strip")
    strip_count = lax.axis_size("strip")
    section_count = lax.axis_size("section")
    samples, row_count, flat_width = cotangent.shape
    channels = weights.shape[-1]
    col_count = flat_width // channels
    coarse_rows = row_count * 3 // 4
    coarse_cols = col_count * 3 // 4
    row_table = jnp.array(
        [
            row_count * 3**section_level // 4**section_level
            for section_level in range(section_count)
        ],
        jnp.int32,
    )
    col_table = jnp.array(
        [
            col_count * 3**section_level // 4**section_level
            for section_level in range(section_count)
        ],
        jnp.int32,
    )
    live_rows = row_table[section_id]
    live_cols = col_table[section_id]
    row_index = lax.iota(jnp.int32, row_count)
    col_index = lax.iota(jnp.int32, col_count)
    col_live = col_index < live_cols
    keep_mask = ((row_index < live_rows)[:, None, None] & col_live[None, :, None]).astype(
        jnp.float32
    )
    kernel_in = weights[0, 0]
    kernel_out = weights[0, 1]
    kernel_in_back = flipped(kernel_in)
    kernel_out_back = flipped(kernel_out)
    bias_in = biases[0, 0]
    bias_out = biases[0, 1]
    cot_grid = cotangent.reshape(samples, row_count, col_count, channels)
    act_grid = activations[0].reshape(samples, row_count, col_count, channels)
    group_count = samples // samples
    tick_count = group_count + section_count - 1

    def section_backward(grad_out, field_in):
        got_input = extended_2(edge_rows(field_in, 1, live_rows), (("strip", 1),), 1)
        input_ext = attach(field_in, got_input, 1, live_rows)
        pre_in = conv_rows(input_ext, kernel_in) + bias_in
        hidden = (activate(pre_in) * keep_mask).astype(jnp.bfloat16)
        got_hidden = extended_2(edge_rows(hidden, 1, live_rows), (("strip", 1),), 1)
        hidden_ext = attach(hidden, got_hidden, 1, live_rows)
        pre_out = conv_rows(hidden_ext, kernel_out) + bias_out
        error_out = (grad_out.astype(jnp.float32) * steepness(pre_out) * keep_mask).astype(
            jnp.bfloat16
        )
        got_error = extended_2(edge_rows(error_out, 1, live_rows), (("strip", 1),), 1)
        error_ext = attach(error_out, got_error, 1, live_rows)
        back_hidden = conv_rows(error_ext, kernel_out_back)
        error_in = (back_hidden * steepness(pre_in) * keep_mask).astype(jnp.bfloat16)
        got_inner = extended_2(edge_rows(error_in, 1, live_rows), (("strip", 1),), 1)
        inner_ext = attach(error_in, got_inner, 1, live_rows)
        back_input = conv_rows(inner_ext, kernel_in_back) * keep_mask
        noise_part = back_input.astype(jnp.bfloat16)
        grad_up = (grad_out.astype(jnp.float32) + back_input).astype(jnp.bfloat16)
        kernel_grads = jnp.stack(
            [weight_taps(input_ext, error_in), weight_taps(hidden_ext, error_out)]
        )
        bias_grads = jnp.stack(
            [
                jnp.sum(error_in, axis=(0, 1, 2), dtype=jnp.float32),
                jnp.sum(error_out, axis=(0, 1, 2), dtype=jnp.float32),
            ]
        )
        return (noise_part, grad_up, kernel_grads, bias_grads)

    def coarse_grad(grad_up, fine_level):
        coarse_level = jnp.minimum(fine_level + 1, section_count - 1)
        fine_height = row_table[fine_level]
        coarse_height = row_table[coarse_level]
        fine_width = col_table[fine_level]
        coarse_width = col_table[coarse_level]
        global_row = strip_id * fine_height + row_index
        row_num = jnp.maximum(6 * global_row - 1, 0)
        row_low = row_num // 8
        row_frac = (row_num - 8 * row_low).astype(jnp.float32) / 8.0
        row_high = jnp.minimum(row_low + 1, strip_count * coarse_height - 1)
        row_on = (row_index < fine_height).astype(jnp.float32)
        base_row = strip_id * coarse_height - 1
        target_row = lax.iota(jnp.int32, coarse_rows + 2)[:, None]
        row_matrix = (
            jnp.where(target_row == (row_low - base_row)[None, :], 1.0 - row_frac[None, :], 0.0)
            + jnp.where(target_row == (row_high - base_row)[None, :], row_frac[None, :], 0.0)
        ) * row_on[None, :]
        col_num = jnp.maximum((2 * col_index + 1) * coarse_width - fine_width, 0)
        col_den = 2 * fine_width
        col_low = col_num // col_den
        col_frac = (col_num - col_den * col_low).astype(jnp.float32) / col_den.astype(jnp.float32)
        col_high = jnp.minimum(col_low + 1, coarse_width - 1)
        col_on = (col_index < fine_width).astype(jnp.float32)
        target_col = lax.iota(jnp.int32, coarse_cols)[:, None]
        col_matrix = (
            jnp.where(target_col == col_low[None, :], 1.0 - col_frac[None, :], 0.0)
            + jnp.where(target_col == col_high[None, :], col_frac[None, :], 0.0)
        ) * col_on[None, :]
        wide_grad = grad_up.astype(jnp.float32)
        partial_cols = jnp.einsum(
            "gyxc,kx->gykc", wide_grad, col_matrix, precision=lax.Precision.HIGHEST
        )
        summed = jnp.einsum(
            "ry,gykc->grkc", row_matrix, partial_cols, precision=lax.Precision.HIGHEST
        )
        rim_pair = jnp.concatenate(
            [summed[:, :1], lax.dynamic_slice_in_dim(summed, coarse_height + 1, 1, 1)], axis=1
        )
        got_rims = extended_2(rim_pair, (("strip", 1),), 1)
        core_rows = summed[:, 1 : coarse_rows + 1]
        index_row = lax.iota(jnp.int32, coarse_rows)[None, :, None, None]
        core_rows = (
            core_rows
            + jnp.where(index_row == 0, got_rims[:, :1], 0.0)
            + jnp.where(index_row == coarse_height - 1, got_rims[:, 3:], 0.0)
        )
        coarse_mask = (
            (lax.iota(jnp.int32, coarse_rows) < coarse_height)[:, None, None]
            & (lax.iota(jnp.int32, coarse_cols) < coarse_width)[None, :, None]
        ).astype(jnp.float32)
        return (core_rows * coarse_mask).astype(jnp.bfloat16)

    def expand(coarse):
        return jnp.pad(
            coarse, ((0, 0), (0, row_count - coarse_rows), (0, col_count - coarse_cols), (0, 0))
        )

    def one_tick(tick_index, state_in):
        incoming, noise_acc, kernel_acc, bias_acc = state_in
        group_index = tick_index - section_id
        active = (group_index >= 0) & (group_index < group_count)
        start_row = jnp.clip(group_index, 0, group_count - 1) * samples
        grad_out = jnp.where(section_id == 0, cot_grid, incoming)
        field_in = (act_grid.astype(jnp.float32) * keep_mask).astype(jnp.bfloat16)
        noise_part, grad_up, kernel_grads, bias_grads = section_backward(grad_out, field_in)
        shifted = shifted_2(grad_up, "section", 1)
        next_in = expand(coarse_grad(shifted, jnp.maximum(section_id - 1, 0)))
        old_noise = noise_acc
        noise_acc = lax.dynamic_update_slice_in_dim(
            noise_acc, jnp.where(active, noise_part, old_noise), start_row, 0
        )
        weight_on = active.astype(jnp.float32)
        return (
            next_in,
            noise_acc,
            kernel_acc + weight_on * kernel_grads,
            bias_acc + weight_on * bias_grads,
        )

    initial = (
        jnp.zeros((samples, row_count, col_count, channels), jnp.bfloat16),
        jnp.zeros((samples, row_count, col_count, channels), jnp.bfloat16),
        jnp.zeros((2, 3, 3, channels, channels), jnp.float32),
        jnp.zeros((2, channels), jnp.float32),
    )
    final_state = lax.fori_loop(0, tick_count, one_tick, initial)
    noise_acc = final_state[1]
    flat = jnp.concatenate([final_state[2].reshape(-1), final_state[3].reshape(-1)])
    taps = flat.shape[0]
    flat = jnp.pad(flat, (0, PACKED * 128 - taps)).reshape(PACKED, 128)
    flat = strip_sum(flat).reshape(-1)
    kernel_sum = flat[: taps - 2 * channels].reshape(final_state[2].shape)
    bias_sum = flat[taps - 2 * channels : taps].reshape(2, channels)
    pixel_count = (samples * strip_count * live_rows * live_cols).astype(jnp.float32)
    scale_back = 1.0 / jnp.sqrt(pixel_count)
    return (
        noise_acc.reshape(1, samples, row_count, flat_width),
        (kernel_sum * scale_back)[None],
        (bias_sum * scale_back)[None],
    )


def solution(mesh):
    return jax.shard_map(
        local,
        mesh=mesh,
        in_specs=(
            P(None, "strip", None),
            P("section", None, "strip", None),
            P("section", None, None, None, None, None),
            P("section", None, None),
        ),
        out_specs=(
            P("section", None, "strip", None),
            P("section", None, None, None, None, None),
            P("section", None, None),
        ),
        check_vma=False,
    )
```

```python
import functools
import math

import jax
import jax.numpy as jnp
from jax import lax
from jax.experimental import pallas as pl
from jax.experimental.pallas import tpu as pltpu
from jax.sharding import PartitionSpec as P

LEAK = 0.05
RING = 8
PIECE = 40
HALF = RING * PIECE
PACKED = 2 * HALF
MESH = pl.DeviceIdType.MESH


def reduce_body(
    src, out, pair_in, y_sum, y_in, z_out, z_in, gathered,
    pair_send, pair_recv, y_send, y_recv, z_send, z_recv, g_send, g_recv, p_send, p_recv,
):
    strip = lax.axis_index("strip")
    core = lax.rem(strip, 2)
    row = lax.rem(lax.div(strip, 2), RING)
    deep = lax.div(strip, 2 * RING)
    partner = strip + 1 - 2 * core

    def y_peer(step):
        return (deep * RING + lax.rem(row + step, RING)) * 2 + core

    def z_peer(step):
        return (lax.rem(deep + step, RING) * RING + row) * 2 + core

    def remote(src_ref, dst_ref, send, recv, strip_id):
        return pltpu.make_async_remote_copy(
            src_ref=src_ref,
            dst_ref=dst_ref,
            send_sem=send,
            recv_sem=recv,
            device_id=(lax.axis_index("section"), strip_id),
            device_id_type=MESH,
        )

    barrier = pltpu.get_barrier_semaphore()
    peers = [partner]
    peers += [y_peer(step) for step in range(1, RING)]
    peers += [z_peer(step) for step in range(1, RING)]
    for peer in peers:
        pl.semaphore_signal(
            barrier,
            inc=1,
            device_id=(lax.axis_index("section"), peer),
            device_id_type=MESH,
        )
    pl.semaphore_wait(barrier, len(peers))

    mine = pl.multiple_of(core * HALF, 8)
    other = pl.multiple_of((1 - core) * HALF, 8)
    swap = remote(src.at[pl.ds(other, HALF)], pair_in, pair_send, pair_recv, partner)
    swap.start()
    swap.wait()
    y_sum[...] = src[pl.ds(mine, HALF), :] + pair_in[...]

    def piece(ref, index):
        return ref.at[pl.ds(pl.multiple_of(index * PIECE, 8), PIECE)]

    scatter = []
    for step in range(1, RING):
        copy = remote(
            piece(y_sum, lax.rem(row + step, RING)),
            y_in.at[step - 1],
            y_send.at[step - 1],
            y_recv.at[step - 1],
            y_peer(step),
        )
        copy.start()
        scatter.append(copy)
    total = y_sum[pl.ds(pl.multiple_of(row * PIECE, 8), PIECE), :]
    for step in range(1, RING):
        scatter[step - 1].wait_recv()
        total = total + y_in[step - 1]
    z_out[...] = total
    z_in[deep] = total
    trade = []
    for step in range(1, RING):
        copy = remote(
            z_out, z_in.at[deep], z_send.at[step - 1], z_recv.at[step - 1], z_peer(step)
        )
        copy.start()
        trade.append(copy)
    for copy in trade:
        copy.wait_recv()
    total = z_in[0]
    for index in range(1, RING):
        total = total + z_in[index]
    own = core * RING + row
    gathered[pl.ds(pl.multiple_of(own * PIECE, 8), PIECE), :] = total
    gather = []
    for step in range(1, RING):
        copy = remote(
            piece(gathered, own),
            piece(gathered, own),
            g_send.at[step - 1],
            g_recv.at[step - 1],
            y_peer(step),
        )
        copy.start()
        gather.append(copy)
    passed = []
    copy = remote(piece(gathered, own), piece(gathered, own), p_send.at[0], p_recv.at[0], partner)
    copy.start()
    passed.append(copy)
    for step in range(1, RING):
        gather[step - 1].wait_recv()
        came = core * RING + lax.rem(row + RING - step, RING)
        copy = remote(
            piece(gathered, came),
            piece(gathered, came),
            p_send.at[step],
            p_recv.at[step],
            partner,
        )
        copy.start()
        passed.append(copy)
    for copy in passed:
        copy.wait_recv()
    out[...] = gathered[...]
    for copy in scatter + trade + gather + passed:
        copy.wait_send()


def strip_sum(packed):
    dma = pltpu.SemaphoreType.DMA
    return pl.pallas_call(
        reduce_body,
        out_shape=jax.ShapeDtypeStruct((PACKED, 128), jnp.float32),
        in_specs=[pl.BlockSpec(memory_space=pltpu.VMEM)],
        out_specs=pl.BlockSpec(memory_space=pltpu.VMEM),
        scratch_shapes=[
            pltpu.VMEM((HALF, 128), jnp.float32),
            pltpu.VMEM((HALF, 128), jnp.float32),
            pltpu.VMEM((RING - 1, PIECE, 128), jnp.float32),
            pltpu.VMEM((PIECE, 128), jnp.float32),
            pltpu.VMEM((RING, PIECE, 128), jnp.float32),
            pltpu.VMEM((PACKED, 128), jnp.float32),
            dma, dma,
            dma((RING - 1,)), dma((RING - 1,)),
            dma((RING - 1,)), dma((RING - 1,)),
            dma((RING - 1,)), dma((RING - 1,)),
            dma((RING,)), dma((RING,)),
        ],
        compiler_params=pltpu.CompilerParams(collective_id=1, has_side_effects=True),
    )(packed)


SECTIONS = 4
ROWS = 64
COLS = 32
CH = 64
GROUP = 4 * CH
SIDE = 2 * CH
BLOCK = 32
NARROW = 16


def plans():
    reach = [0] * SECTIONS
    for level in reversed(range(SECTIONS - 1)):
        reach[level] = (8 * (reach[level + 1] + 2) + 7) // 6
    result = []
    for level in range(SECTIONS):
        rows = ROWS * 3**level // 4**level
        cols = COLS * 3**level // 4**level
        halo = reach[level] + 4
        lead = -(-halo // 8) * 8
        tall = -(-(lead + rows + halo) // 16) * 16
        first = max(0, (rows - halo) // 16 * 16)
        first = min(first, ROWS - BLOCK)
        if rows - first > BLOCK:
            first += 16
        result.append(
            dict(
                rows=rows,
                cols=cols,
                reach=reach[level],
                halo=halo,
                lead=lead,
                tall=tall,
                groups=-(-cols // 4),
                first=first,
            )
        )
    return result


PLANS = plans()
TALL = max(plan["tall"] for plan in PLANS)
WIDE = max(plan["groups"] for plan in PLANS) * GROUP
NEXT_TALL = max(plan["tall"] for plan in PLANS[1:])
NEXT_WIDE = max(plan["groups"] for plan in PLANS[1:]) * GROUP
DEEP = max(plan["tall"] * plan["groups"] for plan in PLANS)


def column_weights(level):
    fine, coarse = PLANS[level]["cols"], PLANS[level + 1]["cols"]
    table = {}
    for col in range(fine):
        num = max((2 * col + 1) * coarse - fine, 0)
        low = num // (2 * fine)
        frac = (num - 2 * fine * low) / (2 * fine)
        high = min(low + 1, coarse - 1)
        table[col, low] = table.get((col, low), 0.0) + 1.0 - frac
        table[col, high] = table.get((col, high), 0.0) + frac
    return {key: value for key, value in table.items() if value != 0.0}


def column_windows(level):
    table = column_weights(level)
    limit = PLANS[level]["groups"] * 4 - 8
    starts = []
    for group in range(PLANS[level + 1]["groups"]):
        used = [fine for fine, coarse in table if coarse // 4 == group]
        start = min(min(used) // 2 * 2, limit)
        assert max(used) < start + 8
        starts.append(start)
    return starts


def iota(shape, axis):
    return lax.broadcasted_iota(jnp.int32, shape, axis)


def mat(left, right):
    return jnp.dot(left, right, preferred_element_type=jnp.float32)


def one_hot(cond):
    return jnp.where(cond, 1.0, 0.0).astype(jnp.bfloat16)


def each_group(count, body):
    step = 2 if count % 2 == 0 else 1

    def run(index, carry):
        for extra in range(step):
            body(index * step + extra)
        return carry

    lax.fori_loop(0, count // step, run, 0)


def lanes(start, size):
    return pl.ds(pl.multiple_of(start, 128), size)


def chain_body(
    x, cot, taps, bias, noise, packed,
    stack, stack_g, bands, x_b, h_b, eo_b, ei_b, slope_in, slope_out, g_b, back_b, up_b,
    row_b, g_out, g_in, cols_m, tall_x, tall_e, grid_a, bias_acc,
    x_send, x_recv, c_send, c_recv, g_send, g_recv,
):
    section = lax.axis_index("section")
    strip = lax.axis_index("strip")
    strips = lax.axis_size("strip")
    below = lax.rem(strip + 1, strips)
    above = lax.rem(strip + strips - 1, strips)
    coarser = lax.rem(section + 1, SECTIONS)
    finer = lax.rem(section + SECTIONS - 1, SECTIONS)

    barrier = pltpu.get_barrier_semaphore()
    for peer in ((section, below), (section, above), (coarser, strip), (finer, strip)):
        pl.semaphore_signal(barrier, inc=1, device_id=peer, device_id_type=MESH)
    pl.semaphore_wait(barrier, 4)

    def remote(src_ref, dst_ref, send, recv, peer):
        return pltpu.make_async_remote_copy(
            src_ref=src_ref,
            dst_ref=dst_ref,
            send_sem=send,
            recv_sem=recv,
            device_id=peer,
            device_id_type=MESH,
        )

    first = PLANS[0]["first"]
    for level in range(1, SECTIONS):
        first = jnp.where(section >= level, PLANS[level]["first"], first)
    x_down = remote(
        x.at[pl.ds(pl.multiple_of(first, 16), BLOCK)],
        stack.at[pl.ds(0, BLOCK)],
        x_send.at[0],
        x_recv.at[0],
        (section, below),
    )
    x_up = remote(
        x.at[pl.ds(0, BLOCK)],
        stack.at[pl.ds(BLOCK + ROWS, BLOCK)],
        x_send.at[1],
        x_recv.at[1],
        (section, above),
    )
    c_down = remote(
        cot.at[pl.ds(ROWS - NARROW, NARROW)],
        stack_g.at[pl.ds(0, NARROW)],
        c_send.at[0],
        c_recv.at[0],
        (section, below),
    )
    c_up = remote(
        cot.at[pl.ds(0, NARROW)],
        stack_g.at[pl.ds(NARROW + ROWS, NARROW)],
        c_send.at[1],
        c_recv.at[1],
        (section, above),
    )
    x_down.start()
    x_up.start()

    @pl.when(section == 0)
    def _():
        c_down.start()
        c_up.start()

    stack[BLOCK : BLOCK + ROWS, :] = x[...]
    stack_g[NARROW : NARROW + ROWS, :] = cot[...]
    bands[...] = jnp.zeros_like(bands)
    for which in range(4):
        for dy in range(3):
            for half in range(2):
                bands[
                    which,
                    SIDE * half + CH : SIDE * half + CH + 4 * CH,
                    GROUP * dy + SIDE * half : GROUP * dy + SIDE * half + SIDE,
                ] = taps[which, dy]

    def hop(level):
        tall = PLANS[level]["tall"]
        width = PLANS[level]["groups"] * GROUP
        part = (pl.ds(0, tall), pl.ds(0, width))
        return g_out.at[part], g_in.at[part], g_send, g_recv

    def run_section(level):
        plan = PLANS[level]
        rows, cols, lead, tall = plan["rows"], plan["cols"], plan["lead"], plan["tall"]
        groups = plan["groups"]
        image = iota((tall, GROUP), 0) - lead
        keep_rows = ((image >= 0) | (strip > 0)) & ((image < rows) | (strip < strips - 1))
        inner_rows = (image >= 0) & (image < rows)
        lane = iota((tall, GROUP), 1)

        def live(group):
            return lane + group * GROUP < cols * CH

        def put(ref, group, value):
            ref[0:tall, lanes(SIDE + group * GROUP, GROUP)] = value.astype(jnp.bfloat16)

        for ref in (x_b, h_b, eo_b, ei_b):
            zero = jnp.zeros((tall, SIDE), jnp.bfloat16)
            ref[0:tall, 0:SIDE] = zero
            ref[0:tall, SIDE + groups * GROUP : 2 * SIDE + groups * GROUP] = zero

        if level + 1 < SECTIONS:
            table = column_weights(level)
            across = iota((CH, SIDE), 1) - iota((CH, SIDE), 0)
            for group, start in enumerate(column_windows(level)):
                for fine in range(8):
                    for half in range(2):
                        coarse = 4 * group + 2 * half
                        low = table.get((start + fine, coarse), 0.0)
                        high = table.get((start + fine, coarse + 1), 0.0)
                        block = jnp.where(across == 0, low, 0.0) + jnp.where(
                            across == CH, high, 0.0
                        )
                        cols_m[
                            group,
                            CH * fine : CH * fine + CH,
                            SIDE * half : SIDE * half + SIDE,
                        ] = block.astype(jnp.bfloat16)

        def conv(ref, which, group):
            window = ref[0:tall, lanes(group * GROUP, 2 * GROUP)]
            three = mat(window, bands[which])
            return (
                pltpu.roll(three[:, :GROUP], 1, 0)
                + three[:, GROUP : 2 * GROUP]
                + pltpu.roll(three[:, 2 * GROUP :], tall - 1, 0)
            )

        x_down.wait_recv()
        x_up.wait_recv()
        span = 2 * BLOCK + ROWS
        at = iota((tall, span), 0) - lead
        slot = iota((tall, span), 1)
        want = jnp.where(
            at < 0,
            at + rows - plan["first"],
            jnp.where(at < rows, at + BLOCK, at - rows + BLOCK + ROWS),
        )
        near = (at >= -plan["halo"]) & (at < rows + plan["halo"])
        near = near & ((at >= 0) | (strip > 0)) & ((at < rows) | (strip < strips - 1))
        pick = one_hot((slot == want) & near)

        def load_x(group):
            value = mat(pick, stack[:, lanes(group * GROUP, GROUP)])
            put(x_b, group, jnp.where(live(group), value, 0.0))

        each_group(groups, load_x)

        def forward_in(group):
            value = conv(x_b, 0, group) + bias[0:1, :]
            small = jnp.exp(-jnp.abs(value))
            soft = jnp.maximum(value, 0.0) + jnp.log1p(small)
            sigmoid = jnp.where(value >= 0.0, 1.0, small) / (1.0 + small)
            hidden = LEAK * value + (1.0 - LEAK) * soft
            keep = keep_rows & live(group)
            put(h_b, group, jnp.where(keep, hidden, 0.0))
            slope = jnp.where(keep, LEAK + (1.0 - LEAK) * sigmoid, 0.0)
            slope_in[0:tall, lanes(group * GROUP, GROUP)] = slope

        each_group(groups, forward_in)

        def forward_out(group):
            value = conv(h_b, 1, group) + bias[1:2, :]
            small = jnp.exp(-jnp.abs(value))
            sigmoid = jnp.where(value >= 0.0, 1.0, small) / (1.0 + small)
            slope = jnp.where(live(group), LEAK + (1.0 - LEAK) * sigmoid, 0.0)
            slope_out[0:tall, lanes(group * GROUP, GROUP)] = slope

        each_group(groups, forward_out)

        if level == 0:
            c_down.wait_recv()
            c_up.wait_recv()
            span_g = 2 * NARROW + ROWS
            at_g = iota((tall, span_g), 0) - lead
            near_g = ((at_g >= 0) | (strip > 0)) & ((at_g < rows) | (strip < strips - 1))
            pick_g = one_hot((iota((tall, span_g), 1) == at_g + NARROW) & near_g)

            def load_g(group):
                span_lanes = lanes(group * GROUP, GROUP)
                g_b[0:tall, span_lanes] = mat(pick_g, stack_g[:, span_lanes])

            each_group(groups, load_g)
        else:
            remote(*hop(level), (finer, strip)).wait_recv()

            def load_g(group):
                span_lanes = lanes(group * GROUP, GROUP)
                g_b[0:tall, span_lanes] = g_in[0:tall, span_lanes].astype(jnp.float32)

            each_group(groups, load_g)

        def error_out(group):
            span_lanes = lanes(group * GROUP, GROUP)
            put(eo_b, group, g_b[0:tall, span_lanes] * slope_out[0:tall, span_lanes])

        each_group(groups, error_out)

        def error_in(group):
            value = conv(eo_b, 2, group)
            put(ei_b, group, value * slope_in[0:tall, lanes(group * GROUP, GROUP)])

        each_group(groups, error_in)

        def back_input(group):
            span_lanes = lanes(group * GROUP, GROUP)
            value = jnp.where(live(group), conv(ei_b, 3, group), 0.0)
            back_b[0:tall, span_lanes] = value.astype(jnp.bfloat16)
            total = g_b[0:tall, span_lanes] + value
            up_b[0:tall, span_lanes] = total.astype(jnp.bfloat16)

        each_group(groups, back_input)

        if level + 1 < SECTIONS:
            after = PLANS[level + 1]
            shape = (after["tall"], tall)
            coarse_row = strip * after["rows"] + iota(shape, 0) - after["lead"]
            local_row = iota(shape, 1) - lead
            fine_row = strip * rows + local_row
            num = jnp.maximum(6 * fine_row - 1, 0)
            low = num >> 3
            frac = (num & 7).astype(jnp.float32) * 0.125
            high = jnp.minimum(low + 1, strips * after["rows"] - 1)
            real = (fine_row >= 0) & (fine_row < strips * rows)
            real = real & (local_row >= -plan["reach"]) & (local_row < rows + plan["reach"])
            real = real & (coarse_row >= 0) & (coarse_row < strips * after["rows"])
            row_m = jnp.where(coarse_row == low, 1.0 - frac, 0.0)
            row_m = row_m + jnp.where(coarse_row == high, frac, 0.0)
            row_m = jnp.where(real, row_m, 0.0).astype(jnp.bfloat16)

            def rows_down(group):
                span_lanes = lanes(group * GROUP, GROUP)
                value = mat(row_m, up_b[0:tall, span_lanes])
                row_b[0 : after["tall"], span_lanes] = value.astype(jnp.bfloat16)

            each_group(groups, rows_down)
            for group, start in enumerate(column_windows(level)):
                value = mat(
                    row_b[0 : after["tall"], CH * start : CH * start + 2 * GROUP],
                    cols_m[group],
                )
                g_out[0 : after["tall"], GROUP * group : GROUP * group + GROUP] = value.astype(
                    jnp.bfloat16
                )
            remote(*hop(level + 1), (coarser, strip)).start()

        choose = one_hot(
            (iota((ROWS, tall), 1) == iota((ROWS, tall), 0) + lead)
            & (iota((ROWS, tall), 0) < rows)
        )

        def save(group):
            span_lanes = lanes(group * GROUP, GROUP)
            noise[:, span_lanes] = mat(choose, back_b[0:tall, span_lanes]).astype(jnp.bfloat16)

        each_group(groups, save)
        if groups * GROUP < COLS * CH:
            noise[:, groups * GROUP :] = jnp.zeros(
                (ROWS, COLS * CH - groups * GROUP), jnp.bfloat16
            )

        for which, (field, error) in enumerate(((x_b, ei_b), (h_b, eo_b))):
            bias_acc[which : which + 1, :] = jnp.zeros((1, GROUP), jnp.float32)

            def pile(group):
                where_rows = pl.ds(pl.multiple_of(group * tall, 16), tall)
                tall_x[where_rows, :] = field[0:tall, lanes(group * GROUP, 2 * GROUP)]
                value = error[0:tall, lanes(SIDE + group * GROUP, GROUP)].astype(jnp.float32)
                value = jnp.where(inner_rows, value, 0.0)
                bias_acc[which : which + 1, :] += jnp.sum(value, axis=0, keepdims=True)
                tall_e[where_rows, 0:GROUP] = pltpu.roll(value, tall - 1, 0).astype(jnp.bfloat16)
                tall_e[where_rows, GROUP : 2 * GROUP] = value.astype(jnp.bfloat16)
                tall_e[where_rows, 2 * GROUP :] = pltpu.roll(value, 1, 0).astype(jnp.bfloat16)

            each_group(groups, pile)
            grid_a[which] = lax.dot_general(
                tall_x[0 : groups * tall, :],
                tall_e[0 : groups * tall, :],
                (((0,), (0,)), ((), ())),
                preferred_element_type=jnp.float32,
            )

    for level in range(SECTIONS):
        pl.when(section == level)(functools.partial(run_section, level))

    def folded(which, tap):
        dy, dx = tap // 3, tap % 3
        low, high = 0.0, 0.0
        for half in range(2):
            span_lanes = slice(GROUP * dy + SIDE * half, GROUP * dy + SIDE * half + SIDE)
            row = CH * (2 * half + dx + 1)
            low = low + grid_a[which, row : row + CH, span_lanes]
            high = high + grid_a[which, row + CH : row + 2 * CH, span_lanes]
        return low, high

    left = iota((CH, SIDE), 1) < CH
    for pair in range(9):
        low_a, high_a = folded((2 * pair) // 9, (2 * pair) % 9)
        low_b, high_b = folded((2 * pair + 1) // 9, (2 * pair + 1) % 9)
        packed[CH * pair : CH * pair + CH, :] = jnp.where(
            left, low_a + pltpu.roll(high_a, CH, 1), high_b + pltpu.roll(low_b, CH, 1)
        )
    sums = bias_acc[:, 0:SIDE] + bias_acc[:, SIDE:]
    sums = sums + pltpu.roll(sums, CH, 1)
    tail = jnp.where(iota((8, SIDE), 1) < CH, sums[0:1, :], sums[1:2, :])
    packed[9 * CH : 9 * CH + 8, :] = jnp.where(iota((8, SIDE), 0) == 0, tail, 0.0)
    packed[9 * CH + 8 :, :] = jnp.zeros((PACKED - 9 * CH - 8, SIDE), jnp.float32)

    x_down.wait_send()
    x_up.wait_send()

    @pl.when(section == 0)
    def _():
        c_down.wait_send()
        c_up.wait_send()

    for level in range(1, SECTIONS):

        @pl.when(section == level - 1)
        def _():
            remote(*hop(level), (coarser, strip)).wait_send()


def chain(x, cot, taps, bias):
    dma = pltpu.SemaphoreType.DMA
    half, full = jnp.bfloat16, jnp.float32
    padded = WIDE + 2 * SIDE
    in_vmem = pl.BlockSpec(memory_space=pltpu.VMEM)
    return pl.pallas_call(
        chain_body,
        out_shape=(
            jax.ShapeDtypeStruct((ROWS, COLS * CH), half),
            jax.ShapeDtypeStruct((PACKED, 128), full),
        ),
        in_specs=[in_vmem] * 4,
        out_specs=(in_vmem, in_vmem),
        scratch_shapes=[
            pltpu.VMEM((2 * BLOCK + ROWS, COLS * CH), half),
            pltpu.VMEM((2 * NARROW + ROWS, COLS * CH), half),
            pltpu.VMEM((4, 2 * GROUP, 3 * GROUP), half),
            pltpu.VMEM((TALL, padded), half),
            pltpu.VMEM((TALL, padded), half),
            pltpu.VMEM((TALL, padded), half),
            pltpu.VMEM((TALL, padded), half),
            pltpu.VMEM((TALL, WIDE), full),
            pltpu.VMEM((TALL, WIDE), full),
            pltpu.VMEM((TALL, WIDE), full),
            pltpu.VMEM((TALL, WIDE), half),
            pltpu.VMEM((TALL, WIDE), half),
            pltpu.VMEM((NEXT_TALL, WIDE), half),
            pltpu.VMEM((NEXT_TALL, NEXT_WIDE), half),
            pltpu.VMEM((NEXT_TALL, NEXT_WIDE), half),
            pltpu.VMEM((NEXT_WIDE // GROUP, 2 * GROUP, GROUP), half),
            pltpu.VMEM((DEEP, 2 * GROUP), half),
            pltpu.VMEM((DEEP, 3 * GROUP), half),
            pltpu.VMEM((2, 2 * GROUP, 3 * GROUP), full),
            pltpu.VMEM((2, GROUP), full),
            dma((2,)), dma((2,)), dma((2,)), dma((2,)), dma, dma,
        ],
        compiler_params=pltpu.CompilerParams(
            collective_id=0, has_side_effects=True, vmem_limit_bytes=48 << 20
        ),
    )(x, cot, taps, bias)


def flipped(kernel):
    return jnp.transpose(kernel[::-1, ::-1], (0, 1, 3, 2))


def local(cotangent, activations, weights, biases):
    section = lax.axis_index("section")
    strips = lax.axis_size("strip")
    kernel_in, kernel_out = weights[0, 0], weights[0, 1]
    taps = jnp.stack([kernel_in, kernel_out, flipped(kernel_out), flipped(kernel_in)])
    taps = taps.reshape(4, 3, 3 * CH, CH)
    edge = ((0, 0), (0, 0))
    taps = jnp.concatenate(
        [
            jnp.pad(taps, edge + ((0, CH), (0, 0))),
            jnp.pad(taps, edge + ((CH, 0), (0, 0))),
        ],
        axis=-1,
    )
    bias = jnp.tile(biases[0], (1, 4))
    noise, packed = chain(activations[0, 0], cotangent[0], taps, bias)
    total = strip_sum(packed)
    scales = jnp.array(
        [1.0 / math.sqrt(strips * plan["rows"] * plan["cols"]) for plan in PLANS], jnp.float32
    )
    total = total * scales[section]
    kernel_grads = total[: 9 * CH].reshape(9, CH, 2, CH).transpose(0, 2, 1, 3)
    return (
        noise[None, None],
        kernel_grads.reshape(1, 2, 3, 3, CH, CH),
        total[9 * CH].reshape(1, 2, CH),
    )

def solution(mesh):
    return jax.shard_map(
        local,
        mesh=mesh,
        in_specs=(
            P(None, "strip", None),
            P("section", None, "strip", None),
            P("section", None, None, None, None, None),
            P("section", None, None),
        ),
        out_specs=(
            P("section", None, "strip", None),
            P("section", None, None, None, None, None),
            P("section", None, None),
        ),
        check_vma=False,
    )
```

```python
import math

import jax
import jax.numpy as jnp
from jax import lax
from jax.experimental import pallas as pl
from jax.experimental.pallas import tpu as pltpu
from jax.sharding import PartitionSpec as P

LEAK = 0.05
RING = 8
PIECE = 40
PIECES = 2 * RING
MESH = pl.DeviceIdType.MESH


def sum_peers(strip):
    core = lax.rem(strip, 2)
    row = lax.rem(lax.div(strip, 2), RING)
    deep = lax.div(strip, 2 * RING)
    partner = strip + 1 - 2 * core
    along_y = [(deep * RING + lax.rem(row + step, RING)) * 2 + core for step in range(1, RING)]
    along_z = [(lax.rem(deep + step, RING) * RING + row) * 2 + core for step in range(1, RING)]
    return core, row, deep, partner, along_y, along_z


def strip_sum(
    remote, strip, scale, meanwhile, src, pair_in, y_sum, y_out, y_in, z_out, z_in, gathered,
    pair_send, pair_recv, y_send, y_recv, z_send, z_recv, g_send, g_recv, p_send, p_recv,
):
    core, row, deep, partner, along_y, along_z = sum_peers(strip)
    mine = core * RING
    swap = remote(
        src.at[pl.ds((1 - core) * RING, RING)], pair_in, pair_send, pair_recv, partner
    )
    swap.start()
    swap.wait()
    both = src[pl.ds(mine, RING)] + pair_in[...]
    y_sum[...] = both
    y_out[...] = both.astype(jnp.bfloat16)
    scatter = []
    for step in range(1, RING):
        copy = remote(
            y_out.at[lax.rem(row + step, RING)],
            y_in.at[step - 1],
            y_send.at[step - 1],
            y_recv.at[step - 1],
            along_y[step - 1],
        )
        copy.start()
        scatter.append(copy)
    meanwhile()
    total = y_sum[row]
    for step in range(1, RING):
        scatter[step - 1].wait_recv()
        total = total + y_in[step - 1].astype(jnp.float32)
    z_out[...] = total.astype(jnp.bfloat16)
    z_in[deep] = total.astype(jnp.bfloat16)
    trade = []
    for step in range(1, RING):
        copy = remote(
            z_out, z_in.at[deep], z_send.at[step - 1], z_recv.at[step - 1], along_z[step - 1]
        )
        copy.start()
        trade.append(copy)
    for copy in trade:
        copy.wait_recv()
    total = z_in[0].astype(jnp.float32)
    for index in range(1, RING):
        total = total + z_in[index].astype(jnp.float32)
    own = mine + row
    gathered[own] = (total * scale).astype(jnp.bfloat16)
    gather = []
    for step in range(1, RING):
        copy = remote(
            gathered.at[own],
            gathered.at[own],
            g_send.at[step - 1],
            g_recv.at[step - 1],
            along_y[step - 1],
        )
        copy.start()
        gather.append(copy)
    passed = [
        remote(gathered.at[own], gathered.at[own], p_send.at[0], p_recv.at[0], partner)
    ]
    passed[0].start()
    for step in range(1, RING):
        gather[step - 1].wait_recv()
        came = mine + lax.rem(row + RING - step, RING)
        copy = remote(
            gathered.at[came], gathered.at[came], p_send.at[step], p_recv.at[step], partner
        )
        copy.start()
        passed.append(copy)
    for copy in passed:
        copy.wait_recv()
    for copy in scatter + trade + gather + passed:
        copy.wait_send()


SECTIONS = 4
ROWS = 64
COLS = 32
CH = 64
GROUP = 4 * CH
SIDE = 2 * CH
BLOCK = 32
NARROW = 16
CHUNKS = (4, 3, 5, 4)


def plans():
    reach = [0] * SECTIONS
    for level in reversed(range(SECTIONS - 1)):
        reach[level] = (8 * (reach[level + 1] + 2) + 7) // 6
    result = []
    for level in range(SECTIONS):
        rows = ROWS * 3**level // 4**level
        cols = COLS * 3**level // 4**level
        halo = reach[level] + 4
        lead = halo
        tall = -(-(lead + rows + halo) // 16) * 16
        first = max(0, (rows - halo) // 16 * 16)
        first = min(first, ROWS - BLOCK)
        if rows - first > BLOCK:
            first += 16
        result.append(
            dict(
                rows=rows,
                cols=cols,
                reach=reach[level],
                halo=halo,
                lead=lead,
                tall=tall,
                groups=-(-cols // 4),
                first=first,
                sent=-(-(lead + rows + reach[level] + 2) // 8) * 8,
                chunk=CHUNKS[level],
            )
        )
    return result


PLANS = plans()
TALL = max(plan["tall"] for plan in PLANS)
WIDE = max(plan["groups"] for plan in PLANS) * GROUP
NEXT_TALL = max(plan["tall"] for plan in PLANS[1:])
NEXT_WIDE = max(plan["groups"] for plan in PLANS[1:]) * GROUP
DEEP = max(plan["tall"] * plan["groups"] for plan in PLANS)


def column_weights(level):
    fine, coarse = PLANS[level]["cols"], PLANS[level + 1]["cols"]
    table = {}
    for col in range(fine):
        num = max((2 * col + 1) * coarse - fine, 0)
        low = num // (2 * fine)
        frac = (num - 2 * fine * low) / (2 * fine)
        high = min(low + 1, coarse - 1)
        table[col, low] = table.get((col, low), 0.0) + 1.0 - frac
        table[col, high] = table.get((col, high), 0.0) + frac
    return {key: value for key, value in table.items() if value != 0.0}


def column_windows(level):
    table = column_weights(level)
    limit = PLANS[level]["groups"] * 4 - 8
    starts = []
    for group in range(PLANS[level + 1]["groups"]):
        used = [fine for fine, coarse in table if coarse // 4 == group]
        start = min(min(used) // 2 * 2, limit)
        assert max(used) < start + 8
        starts.append(start)
    return starts


def iota(shape, axis):
    return lax.broadcasted_iota(jnp.int32, shape, axis)


def mat(left, right):
    return jnp.dot(left, right, preferred_element_type=jnp.float32)


def one_hot(cond):
    return jnp.where(cond, 1.0, 0.0).astype(jnp.bfloat16)


def each_group(count, body, step):
    def run(index, carry):
        body([index * step + extra for extra in range(step)])
        return carry

    if step == count:
        body(list(range(count)))
    else:
        lax.fori_loop(0, count // step, run, 0)


def lanes(start, size):
    if isinstance(start, int):
        return pl.ds(start, size)
    return pl.ds(pl.multiple_of(start, 128), size)


def chain_body(
    x, cot, taps, bias, noise, kernel_out, bias_out,
    stack, stack_g, bands, x_b, h_b, eo_b, ei_b, slope_in, slope_out, g_b, back_b, up_b,
    row_b, g_out, g_in, cols_m, tall_x, tall_e, grid_a, bias_acc,
    packed, final, x_send, x_recv, c_send, c_recv, g_send, g_recv, *sum_refs,
):
    section = lax.axis_index("section")
    strip = lax.axis_index("strip")
    strips = lax.axis_size("strip")
    below = lax.rem(strip + 1, strips)
    above = lax.rem(strip + strips - 1, strips)
    coarser = lax.rem(section + 1, SECTIONS)
    finer = lax.rem(section + SECTIONS - 1, SECTIONS)

    barrier = pltpu.get_barrier_semaphore()
    partner, along_y, along_z = sum_peers(strip)[3:]
    peers = [(section, below), (section, above), (coarser, strip), (finer, strip)]
    peers += [(section, peer) for peer in [partner] + along_y + along_z]
    for peer in peers:
        pl.semaphore_signal(barrier, inc=1, device_id=peer, device_id_type=MESH)
    pl.semaphore_wait(barrier, len(peers))

    def remote(src_ref, dst_ref, send, recv, peer):
        return pltpu.make_async_remote_copy(
            src_ref=src_ref,
            dst_ref=dst_ref,
            send_sem=send,
            recv_sem=recv,
            device_id=peer,
            device_id_type=MESH,
        )

    first = PLANS[0]["first"]
    for level in range(1, SECTIONS):
        first = jnp.where(section >= level, PLANS[level]["first"], first)
    x_down = remote(
        x.at[pl.ds(pl.multiple_of(first, 16), BLOCK)],
        stack.at[pl.ds(0, BLOCK)],
        x_send.at[0],
        x_recv.at[0],
        (section, below),
    )
    x_up = remote(
        x.at[pl.ds(0, BLOCK)],
        stack.at[pl.ds(BLOCK + ROWS, BLOCK)],
        x_send.at[1],
        x_recv.at[1],
        (section, above),
    )
    c_down = remote(
        cot.at[pl.ds(ROWS - NARROW, NARROW)],
        stack_g.at[pl.ds(0, NARROW)],
        c_send.at[0],
        c_recv.at[0],
        (section, below),
    )
    c_up = remote(
        cot.at[pl.ds(0, NARROW)],
        stack_g.at[pl.ds(NARROW + ROWS, NARROW)],
        c_send.at[1],
        c_recv.at[1],
        (section, above),
    )
    x_down.start()
    x_up.start()

    @pl.when(section == 0)
    def _():
        c_down.start()
        c_up.start()

    stack[BLOCK : BLOCK + ROWS, :] = x[...]
    stack_g[NARROW : NARROW + ROWS, :] = cot[...]
    bands[...] = jnp.zeros_like(bands)
    for which in range(4):
        for dy in range(3):
            for half in range(2):
                bands[
                    which,
                    SIDE * half + CH : SIDE * half + CH + 4 * CH,
                    GROUP * dy + SIDE * half : GROUP * dy + SIDE * half + SIDE,
                ] = taps[which, dy]

    bias_rows = jnp.concatenate([bias[...]] * 4, axis=1)

    def hop(level, group, peer):
        part = (pl.ds(0, PLANS[level]["sent"]), pl.ds(group * GROUP, GROUP))
        return remote(g_out.at[part], g_in.at[part], g_send.at[group], g_recv.at[group], peer)

    def live_of(level, group):
        lane = iota((PLANS[level]["tall"], GROUP), 1)
        return lane + group * GROUP < PLANS[level]["cols"] * CH

    def conv_of(tall, ref, which, group_list):
        windows = [ref[0:tall, lanes(group * GROUP, 2 * GROUP)] for group in group_list]
        three = mat(jnp.concatenate(windows, axis=0), bands[which])
        result = []
        for index in range(len(group_list)):
            part = three[index * tall : (index + 1) * tall]
            result.append(
                pltpu.roll(part[:, :GROUP], 1, 0)
                + part[:, GROUP : 2 * GROUP]
                + pltpu.roll(part[:, 2 * GROUP :], tall - 1, 0)
            )
        return zip(group_list, result)

    def save_noise(level):
        plan = PLANS[level]
        rows, tall, groups = plan["rows"], plan["tall"], plan["groups"]
        shape = (ROWS, tall)
        choose = one_hot(
            (iota(shape, 1) == iota(shape, 0) + plan["lead"]) & (iota(shape, 0) < rows)
        )

        def save(group_list):
            for group in group_list:
                span_lanes = lanes(group * GROUP, GROUP)
                noise[:, span_lanes] = mat(choose, back_b[0:tall, span_lanes]).astype(
                    jnp.bfloat16
                )

        each_group(groups, save, plan["chunk"])
        if groups * GROUP < COLS * CH:
            noise[:, groups * GROUP :] = jnp.zeros(
                (ROWS, COLS * CH - groups * GROUP), jnp.bfloat16
            )

    def finish_last():
        level = SECTIONS - 1
        tall = PLANS[level]["tall"]

        def back_last(group_list):
            for group, value in conv_of(tall, ei_b, 3, group_list):
                value = jnp.where(live_of(level, group), value, 0.0)
                back_b[0:tall, lanes(group * GROUP, GROUP)] = value.astype(jnp.bfloat16)

        each_group(PLANS[level]["groups"], back_last, PLANS[level]["chunk"])
        save_noise(level)

    def run_section(level):
        plan = PLANS[level]
        rows, lead, tall = plan["rows"], plan["lead"], plan["tall"]
        groups, chunk = plan["groups"], plan["chunk"]
        image = iota((tall, GROUP), 0) - lead
        keep_rows = ((image >= 0) | (strip > 0)) & ((image < rows) | (strip < strips - 1))
        inner_rows = (image >= 0) & (image < rows)

        def live(group):
            return live_of(level, group)

        def conv(ref, which, group_list):
            return conv_of(tall, ref, which, group_list)

        def put(ref, group, value):
            ref[0:tall, lanes(SIDE + group * GROUP, GROUP)] = value.astype(jnp.bfloat16)

        for ref in (x_b, h_b, eo_b, ei_b):
            zero = jnp.zeros((tall, SIDE), jnp.bfloat16)
            ref[0:tall, 0:SIDE] = zero
            ref[0:tall, SIDE + groups * GROUP : 2 * SIDE + groups * GROUP] = zero

        if level + 1 < SECTIONS:
            table = column_weights(level)
            across = iota((CH, SIDE), 1) - iota((CH, SIDE), 0)
            for group, start in enumerate(column_windows(level)):
                for fine in range(8):
                    for half in range(2):
                        coarse = 4 * group + 2 * half
                        low = table.get((start + fine, coarse), 0.0)
                        high = table.get((start + fine, coarse + 1), 0.0)
                        block = jnp.where(across == 0, low, 0.0) + jnp.where(
                            across == CH, high, 0.0
                        )
                        cols_m[
                            group,
                            CH * fine : CH * fine + CH,
                            SIDE * half : SIDE * half + SIDE,
                        ] = block.astype(jnp.bfloat16)

        x_down.wait_recv()
        x_up.wait_recv()
        span = 2 * BLOCK + ROWS
        at = iota((tall, span), 0) - lead
        slot = iota((tall, span), 1)
        want = jnp.where(
            at < 0,
            at + rows - plan["first"],
            jnp.where(at < rows, at + BLOCK, at - rows + BLOCK + ROWS),
        )
        near = (at >= -plan["halo"]) & (at < rows + plan["halo"])
        near = near & ((at >= 0) | (strip > 0)) & ((at < rows) | (strip < strips - 1))
        pick = one_hot((slot == want) & near)

        def load_x(group_list):
            for group in group_list:
                value = mat(pick, stack[:, lanes(group * GROUP, GROUP)])
                put(x_b, group, jnp.where(live(group), value, 0.0))

        each_group(groups, load_x, chunk)

        def forward_in(group_list):
            for group, value in conv(x_b, 0, group_list):
                value = value + bias_rows[0:1, :]
                small = jnp.exp(-jnp.abs(value))
                soft = jnp.maximum(value, 0.0) + jnp.log1p(small)
                sigmoid = jnp.where(value >= 0.0, 1.0, small) / (1.0 + small)
                hidden = LEAK * value + (1.0 - LEAK) * soft
                keep = keep_rows & live(group)
                put(h_b, group, jnp.where(keep, hidden, 0.0))
                slope = jnp.where(keep, LEAK + (1.0 - LEAK) * sigmoid, 0.0)
                slope_in[0:tall, lanes(group * GROUP, GROUP)] = slope

        each_group(groups, forward_in, chunk)

        def forward_out(group_list):
            for group, value in conv(h_b, 1, group_list):
                value = value + bias_rows[1:2, :]
                small = jnp.exp(-jnp.abs(value))
                sigmoid = jnp.where(value >= 0.0, 1.0, small) / (1.0 + small)
                slope = jnp.where(live(group), LEAK + (1.0 - LEAK) * sigmoid, 0.0)
                slope_out[0:tall, lanes(group * GROUP, GROUP)] = slope

        each_group(groups, forward_out, chunk)

        if level == 0:
            c_down.wait_recv()
            c_up.wait_recv()
            span_g = 2 * NARROW + ROWS
            at_g = iota((tall, span_g), 0) - lead
            near_g = ((at_g >= 0) | (strip > 0)) & ((at_g < rows) | (strip < strips - 1))
            pick_g = one_hot((iota((tall, span_g), 1) == at_g + NARROW) & near_g)

            def load_g(group_list):
                for group in group_list:
                    span_lanes = lanes(group * GROUP, GROUP)
                    value = mat(pick_g, stack_g[:, span_lanes])
                    g_b[0:tall, span_lanes] = value
                    put(eo_b, group, value * slope_out[0:tall, span_lanes])

            each_group(groups, load_g, chunk)
        else:
            sent = plan["sent"]
            for group in range(groups):
                hop(level, group, (finer, strip)).wait_recv()
                span_lanes = lanes(group * GROUP, GROUP)
                value = g_in[0:sent, span_lanes].astype(jnp.float32)
                if sent < tall:
                    rest = jnp.zeros((tall - sent, GROUP), jnp.float32)
                    value = jnp.concatenate([value, rest], axis=0)
                g_b[0:tall, span_lanes] = value
                put(eo_b, group, value * slope_out[0:tall, span_lanes])

        def error_in(group_list):
            for group, value in conv(eo_b, 2, group_list):
                put(ei_b, group, value * slope_in[0:tall, lanes(group * GROUP, GROUP)])

        each_group(groups, error_in, chunk)

        def back_input(group_list):
            for group, value in conv(ei_b, 3, group_list):
                span_lanes = lanes(group * GROUP, GROUP)
                value = jnp.where(live(group), value, 0.0)
                back_b[0:tall, span_lanes] = value.astype(jnp.bfloat16)
                total = g_b[0:tall, span_lanes] + value
                up_b[0:tall, span_lanes] = total.astype(jnp.bfloat16)

        if level + 1 < SECTIONS:
            after = PLANS[level + 1]
            shape = (after["tall"], tall)
            coarse_row = strip * after["rows"] + iota(shape, 0) - after["lead"]
            local_row = iota(shape, 1) - lead
            fine_row = strip * rows + local_row
            num = jnp.maximum(6 * fine_row - 1, 0)
            low = num >> 3
            frac = (num & 7).astype(jnp.float32) * 0.125
            high = jnp.minimum(low + 1, strips * after["rows"] - 1)
            real = (fine_row >= 0) & (fine_row < strips * rows)
            real = real & (local_row >= -plan["reach"]) & (local_row < rows + plan["reach"])
            real = real & (coarse_row >= 0) & (coarse_row < strips * after["rows"])
            row_m = jnp.where(coarse_row == low, 1.0 - frac, 0.0)
            row_m = row_m + jnp.where(coarse_row == high, frac, 0.0)
            row_m = jnp.where(real, row_m, 0.0).astype(jnp.bfloat16)

            windows = column_windows(level)
            ready = 0
            for begin in range(0, groups, chunk):
                part = list(range(begin, begin + chunk))
                back_input(part)
                for group in part:
                    span_lanes = lanes(group * GROUP, GROUP)
                    value = mat(row_m, up_b[0:tall, span_lanes])
                    row_b[0 : after["tall"], span_lanes] = value.astype(jnp.bfloat16)
                while ready < len(windows) and windows[ready] + 8 <= 4 * (begin + chunk):
                    start = CH * windows[ready]
                    value = mat(
                        row_b[0 : after["tall"], start : start + 2 * GROUP], cols_m[ready]
                    )
                    g_out[0 : after["tall"], GROUP * ready : GROUP * ready + GROUP] = (
                        value.astype(jnp.bfloat16)
                    )
                    hop(level + 1, ready, (coarser, strip)).start()
                    ready += 1
            assert ready == len(windows)

        if level + 1 < SECTIONS:
            save_noise(level)

        for which, (field, error) in enumerate(((x_b, ei_b), (h_b, eo_b))):
            bias_acc[which : which + 1, :] = jnp.zeros((1, GROUP), jnp.float32)

            def pile(group_list):
                for group in group_list:
                    if isinstance(group, int):
                        where_rows = pl.ds(group * tall, tall)
                    else:
                        where_rows = pl.ds(pl.multiple_of(group * tall, 16), tall)
                    tall_x[where_rows, :] = field[0:tall, lanes(group * GROUP, 2 * GROUP)]
                    value = error[0:tall, lanes(SIDE + group * GROUP, GROUP)]
                    value = jnp.where(inner_rows, value.astype(jnp.float32), 0.0)
                    bias_acc[which : which + 1, :] += jnp.sum(value, axis=0, keepdims=True)
                    tall_e[where_rows, 0:GROUP] = pltpu.roll(value, tall - 1, 0).astype(
                        jnp.bfloat16
                    )
                    tall_e[where_rows, GROUP : 2 * GROUP] = value.astype(jnp.bfloat16)
                    tall_e[where_rows, 2 * GROUP :] = pltpu.roll(value, 1, 0).astype(
                        jnp.bfloat16
                    )

            each_group(groups, pile, chunk)
            grid_a[which] = lax.dot_general(
                tall_x[0 : groups * tall, :],
                tall_e[0 : groups * tall, :],
                (((0,), (0,)), ((), ())),
                preferred_element_type=jnp.float32,
            )

    for level in range(SECTIONS):

        @pl.when(section == level)
        def _():
            run_section(level)

    def folded(which, tap):
        dy, dx = tap // 3, tap % 3
        low, high = 0.0, 0.0
        for half in range(2):
            span_lanes = slice(GROUP * dy + SIDE * half, GROUP * dy + SIDE * half + SIDE)
            row = CH * (2 * half + dx + 1)
            low = low + grid_a[which, row : row + CH, span_lanes]
            high = high + grid_a[which, row + CH : row + 2 * CH, span_lanes]
        return low, high

    left = iota((CH, SIDE), 1) < CH
    blocks = []
    for pair in range(9):
        low_a, high_a = folded((2 * pair) // 9, (2 * pair) % 9)
        low_b, high_b = folded((2 * pair + 1) // 9, (2 * pair + 1) % 9)
        blocks.append(
            jnp.where(left, low_a + pltpu.roll(high_a, CH, 1), high_b + pltpu.roll(low_b, CH, 1))
        )
    sums = bias_acc[:, 0:SIDE] + bias_acc[:, SIDE:]
    sums = sums + pltpu.roll(sums, CH, 1)
    tail = jnp.where(iota((8, SIDE), 1) < CH, sums[0:1, :], sums[1:2, :])
    blocks.append(jnp.where(iota((8, SIDE), 0) == 0, tail, 0.0))
    blocks.append(jnp.zeros((PIECES * PIECE - 9 * CH - 8, SIDE), jnp.float32))
    packed[...] = jnp.concatenate(blocks, axis=0).reshape(PIECES, PIECE, SIDE)

    scale = 0.0
    for level, plan in enumerate(PLANS):
        factor = 1.0 / math.sqrt(strips * plan["rows"] * plan["cols"])
        scale = jnp.where(section == level, jnp.float32(factor), scale)

    def meanwhile():
        @pl.when(section == SECTIONS - 1)
        def _():
            finish_last()

    strip_sum(
        lambda a, b, c, d, peer: remote(a, b, c, d, (section, peer)),
        strip,
        scale,
        meanwhile,
        packed,
        *sum_refs,
    )
    gathered = sum_refs[6]
    final[...] = gathered[...].astype(jnp.float32).reshape(PIECES * PIECE, SIDE)
    for pair in range(9):
        block = final[CH * pair : CH * pair + CH, :]
        kernel_out[2 * pair] = block[:, :CH]
        kernel_out[2 * pair + 1] = pltpu.roll(block, CH, 1)[:, :CH]
    sums = final[9 * CH : 9 * CH + 8, :]
    bias_out[0:1, :] = sums[0:1, :CH]
    bias_out[1:2, :] = pltpu.roll(sums, CH, 1)[0:1, :CH]

    x_down.wait_send()
    x_up.wait_send()

    @pl.when(section == 0)
    def _():
        c_down.wait_send()
        c_up.wait_send()

    for level in range(1, SECTIONS):

        @pl.when(section == level - 1)
        def _():
            for group in range(PLANS[level]["groups"]):
                hop(level, group, (coarser, strip)).wait_send()


def chain(x, cot, taps, bias):
    dma = pltpu.SemaphoreType.DMA
    half, full = jnp.bfloat16, jnp.float32
    padded = WIDE + 2 * SIDE
    in_vmem = pl.BlockSpec(memory_space=pltpu.VMEM)
    return pl.pallas_call(
        chain_body,
        out_shape=(
            jax.ShapeDtypeStruct((ROWS, COLS * CH), half),
            jax.ShapeDtypeStruct((18, CH, CH), full),
            jax.ShapeDtypeStruct((2, CH), full),
        ),
        in_specs=[in_vmem] * 4,
        out_specs=(in_vmem, in_vmem, in_vmem),
        scratch_shapes=[
            pltpu.VMEM((2 * BLOCK + ROWS, COLS * CH), half),
            pltpu.VMEM((2 * NARROW + ROWS, COLS * CH), half),
            pltpu.VMEM((4, 2 * GROUP, 3 * GROUP), half),
            pltpu.VMEM((TALL, padded), half),
            pltpu.VMEM((TALL, padded), half),
            pltpu.VMEM((TALL, padded), half),
            pltpu.VMEM((TALL, padded), half),
            pltpu.VMEM((TALL, WIDE), full),
            pltpu.VMEM((TALL, WIDE), full),
            pltpu.VMEM((TALL, WIDE), full),
            pltpu.VMEM((TALL, WIDE), half),
            pltpu.VMEM((TALL, WIDE), half),
            pltpu.VMEM((NEXT_TALL, WIDE), half),
            pltpu.VMEM((NEXT_TALL, NEXT_WIDE), half),
            pltpu.VMEM((NEXT_TALL, NEXT_WIDE), half),
            pltpu.VMEM((NEXT_WIDE // GROUP, 2 * GROUP, GROUP), half),
            pltpu.VMEM((DEEP, 2 * GROUP), half),
            pltpu.VMEM((DEEP, 3 * GROUP), half),
            pltpu.VMEM((2, 2 * GROUP, 3 * GROUP), full),
            pltpu.VMEM((2, GROUP), full),
            pltpu.VMEM((PIECES, PIECE, SIDE), full),
            pltpu.VMEM((PIECES * PIECE, SIDE), full),
            dma((2,)), dma((2,)), dma((2,)), dma((2,)),
            dma((NEXT_WIDE // GROUP,)), dma((NEXT_WIDE // GROUP,)),
            pltpu.VMEM((RING, PIECE, SIDE), full),
            pltpu.VMEM((RING, PIECE, SIDE), full),
            pltpu.VMEM((RING, PIECE, SIDE), half),
            pltpu.VMEM((RING - 1, PIECE, SIDE), half),
            pltpu.VMEM((PIECE, SIDE), half),
            pltpu.VMEM((RING, PIECE, SIDE), half),
            pltpu.VMEM((PIECES, PIECE, SIDE), half),
            dma, dma,
            dma((RING - 1,)), dma((RING - 1,)),
            dma((RING - 1,)), dma((RING - 1,)),
            dma((RING - 1,)), dma((RING - 1,)),
            dma((RING,)), dma((RING,)),
        ],
        compiler_params=pltpu.CompilerParams(
            collective_id=0, has_side_effects=True, vmem_limit_bytes=48 << 20
        ),
    )(x, cot, taps, bias)


def flipped(kernel):
    return jnp.transpose(kernel[::-1, ::-1], (0, 1, 3, 2))


def local(cotangent, activations, weights, biases):
    kernel_in, kernel_out = weights[0, 0], weights[0, 1]
    taps = jnp.stack([kernel_in, kernel_out, flipped(kernel_out), flipped(kernel_in)])
    taps = taps.reshape(4, 3, 3 * CH, CH)
    edge = ((0, 0), (0, 0))
    taps = jnp.concatenate(
        [
            jnp.pad(taps, edge + ((0, CH), (0, 0))),
            jnp.pad(taps, edge + ((CH, 0), (0, 0))),
        ],
        axis=-1,
    )
    noise, kernels, sums = chain(activations[0, 0], cotangent[0], taps, biases[0])
    return (
        noise[None, None],
        kernels.reshape(1, 2, 3, 3, CH, CH),
        sums[None],
    )


def solution(mesh):
    return jax.shard_map(
        local,
        mesh=mesh,
        in_specs=(
            P(None, "strip", None),
            P("section", None, "strip", None),
            P("section", None, None, None, None, None),
            P("section", None, None),
        ),
        out_specs=(
            P("section", None, "strip", None),
            P("section", None, None, None, None, None),
            P("section", None, None),
        ),
        check_vma=False,
    )
```

```python
import math

import jax
import jax.numpy as jnp
from jax import lax
from jax.experimental import pallas as pl
from jax.experimental.pallas import tpu as pltpu
from jax.sharding import PartitionSpec as P

LEAK = 0.05
RING = 8
PIECE = 40
PIECES = 2 * RING
MESH = pl.DeviceIdType.MESH


def sum_peers(strip):
    core = lax.rem(strip, 2)
    row = lax.rem(lax.div(strip, 2), RING)
    deep = lax.div(strip, 2 * RING)
    partner = strip + 1 - 2 * core
    along_y = [(deep * RING + lax.rem(row + step, RING)) * 2 + core for step in range(1, RING)]
    along_z = [(lax.rem(deep + step, RING) * RING + row) * 2 + core for step in range(1, RING)]
    return core, row, deep, partner, along_y, along_z


def strip_sum(
    remote, strip, scale, meanwhile, src, pair_in, y_sum, y_out, y_in, z_out, z_in, gathered,
    pair_send, pair_recv, y_send, y_recv, z_send, z_recv, g_send, g_recv, p_send, p_recv,
):
    core, row, deep, partner, along_y, along_z = sum_peers(strip)
    mine = core * RING
    swap = remote(
        src.at[pl.ds((1 - core) * RING, RING)], pair_in, pair_send, pair_recv, partner
    )
    swap.start()
    swap.wait()
    both = src[pl.ds(mine, RING)] + pair_in[...]
    y_sum[...] = both
    y_out[...] = both.astype(jnp.bfloat16)
    scatter = []
    for step in range(1, RING):
        copy = remote(
            y_out.at[lax.rem(row + step, RING)],
            y_in.at[step - 1],
            y_send.at[step - 1],
            y_recv.at[step - 1],
            along_y[step - 1],
        )
        copy.start()
        scatter.append(copy)
    meanwhile()
    total = y_sum[row]
    for step in range(1, RING):
        scatter[step - 1].wait_recv()
        total = total + y_in[step - 1].astype(jnp.float32)
    z_out[...] = total.astype(jnp.bfloat16)
    z_in[deep] = total.astype(jnp.bfloat16)
    trade = []
    for step in range(1, RING):
        copy = remote(
            z_out, z_in.at[deep], z_send.at[step - 1], z_recv.at[step - 1], along_z[step - 1]
        )
        copy.start()
        trade.append(copy)
    for copy in trade:
        copy.wait_recv()
    total = z_in[0].astype(jnp.float32)
    for index in range(1, RING):
        total = total + z_in[index].astype(jnp.float32)
    own = mine + row
    gathered[own] = (total * scale).astype(jnp.bfloat16)
    gather = []
    for step in range(1, RING):
        copy = remote(
            gathered.at[own],
            gathered.at[own],
            g_send.at[step - 1],
            g_recv.at[step - 1],
            along_y[step - 1],
        )
        copy.start()
        gather.append(copy)
    passed = [
        remote(gathered.at[own], gathered.at[own], p_send.at[0], p_recv.at[0], partner)
    ]
    passed[0].start()
    for step in range(1, RING):
        gather[step - 1].wait_recv()
        came = mine + lax.rem(row + RING - step, RING)
        copy = remote(
            gathered.at[came], gathered.at[came], p_send.at[step], p_recv.at[step], partner
        )
        copy.start()
        passed.append(copy)
    for copy in passed:
        copy.wait_recv()
    for copy in scatter + trade + gather + passed:
        copy.wait_send()


SECTIONS = 4
ROWS = 64
COLS = 32
CH = 64
GROUP = 4 * CH
SIDE = 2 * CH
BLOCK = 32
NARROW = 16
CHUNKS = (4, 3, 5, 4)
LAST_CHUNKS = ((4, 2, 2), (3, 3), (5,))


def plans():
    reach = [0] * SECTIONS
    for level in reversed(range(SECTIONS - 1)):
        reach[level] = (8 * (reach[level + 1] + 2) + 7) // 6
    result = []
    for level in range(SECTIONS):
        rows = ROWS * 3**level // 4**level
        cols = COLS * 3**level // 4**level
        halo = reach[level] + 4
        lead = halo
        tall = -(-(lead + rows + halo) // 16) * 16
        first = max(0, (rows - halo) // 16 * 16)
        first = min(first, ROWS - BLOCK)
        if rows - first > BLOCK:
            first += 16
        result.append(
            dict(
                rows=rows,
                cols=cols,
                reach=reach[level],
                halo=halo,
                lead=lead,
                tall=tall,
                groups=-(-cols // 4),
                first=first,
                sent=-(-(lead + rows + reach[level] + 2) // 8) * 8,
                chunk=CHUNKS[level],
                back=-(-(rows + 2 * halo - 2) // 16) * 16,
            )
        )
    return result


PLANS = plans()
TALL = max(plan["tall"] for plan in PLANS)
WIDE = max(plan["groups"] for plan in PLANS) * GROUP
NEXT_TALL = max(plan["tall"] for plan in PLANS[1:])
NEXT_WIDE = max(plan["groups"] for plan in PLANS[1:]) * GROUP
DEEP = max(plan["back"] * plan["groups"] for plan in PLANS)


def column_weights(level):
    fine, coarse = PLANS[level]["cols"], PLANS[level + 1]["cols"]
    table = {}
    for col in range(fine):
        num = max((2 * col + 1) * coarse - fine, 0)
        low = num // (2 * fine)
        frac = (num - 2 * fine * low) / (2 * fine)
        high = min(low + 1, coarse - 1)
        table[col, low] = table.get((col, low), 0.0) + 1.0 - frac
        table[col, high] = table.get((col, high), 0.0) + frac
    return {key: value for key, value in table.items() if value != 0.0}


def column_windows(level):
    table = column_weights(level)
    limit = PLANS[level]["groups"] * 4 - 8
    starts = []
    for group in range(PLANS[level + 1]["groups"]):
        used = [fine for fine, coarse in table if coarse // 4 == group]
        start = min(min(used) // 2 * 2, limit)
        assert max(used) < start + 8
        starts.append(start)
    return starts


def iota(shape, axis):
    return lax.broadcasted_iota(jnp.int32, shape, axis)


def mat(left, right):
    return jnp.dot(left, right, preferred_element_type=jnp.float32)


def steepness(value):
    half = 0.5 * (1.0 - LEAK)
    return (LEAK + half) + half * jnp.tanh(0.5 * value)


def one_hot(cond):
    return jnp.where(cond, 1.0, 0.0).astype(jnp.bfloat16)


def each_group(count, body, step):
    def run(index, carry):
        body([index * step + extra for extra in range(step)])
        return carry

    if step == count:
        body(list(range(count)))
    else:
        lax.fori_loop(0, count // step, run, 0)


def lanes(start, size):
    if isinstance(start, int):
        return pl.ds(start, size)
    return pl.ds(pl.multiple_of(start, 128), size)


def chain_body(
    x, cot, taps, bias, noise, sums_out,
    stack, stack_g, bands, x_b, h_b, eo_b, ei_b, slope_in, slope_out, g_b, back_b, up_b,
    row_b, g_out, g_in, cols_m, tall_x, tall_e, grid_a, bias_acc,
    packed, x_send, x_recv, c_send, c_recv, g_send, g_recv, *sum_refs,
):
    section = lax.axis_index("section")
    strip = lax.axis_index("strip")
    strips = lax.axis_size("strip")
    below = lax.rem(strip + 1, strips)
    above = lax.rem(strip + strips - 1, strips)
    coarser = lax.rem(section + 1, SECTIONS)
    finer = lax.rem(section + SECTIONS - 1, SECTIONS)

    barrier = pltpu.get_barrier_semaphore()
    partner, along_y, along_z = sum_peers(strip)[3:]
    peers = [(section, below), (section, above), (coarser, strip), (finer, strip)]
    peers += [(section, peer) for peer in [partner] + along_y + along_z]
    for peer in peers:
        pl.semaphore_signal(barrier, inc=1, device_id=peer, device_id_type=MESH)

    bands[...] = jnp.zeros_like(bands)
    blank = jnp.zeros((CH, CH), jnp.float32)
    for which, (source, flip) in enumerate(((0, False), (1, False), (1, True), (0, True))):
        for dy in range(3):
            tap_list = []
            for dx in range(3):
                at = (2 - dy) * 3 + 2 - dx if flip else dy * 3 + dx
                tap_list.append(taps[source, at].astype(jnp.float32))
            tap_list.append(blank)
            for index in range(4):
                pair = (tap_list[index], tap_list[index - 1])
                if flip:
                    block = jnp.concatenate(pair, axis=0).T
                else:
                    block = jnp.concatenate(pair, axis=1)
                block = block.astype(jnp.bfloat16)
                for half in range(2):
                    row = CH * (2 * half + 1 + index)
                    col = GROUP * dy + SIDE * half
                    bands[which, row : row + CH, col : col + SIDE] = block

    pl.semaphore_wait(barrier, len(peers))

    def remote(src_ref, dst_ref, send, recv, peer):
        return pltpu.make_async_remote_copy(
            src_ref=src_ref,
            dst_ref=dst_ref,
            send_sem=send,
            recv_sem=recv,
            device_id=peer,
            device_id_type=MESH,
        )

    first = PLANS[0]["first"]
    for level in range(1, SECTIONS):
        first = jnp.where(section >= level, PLANS[level]["first"], first)
    x_down = remote(
        x.at[pl.ds(pl.multiple_of(first, 16), BLOCK)],
        stack.at[pl.ds(0, BLOCK)],
        x_send.at[0],
        x_recv.at[0],
        (section, below),
    )
    x_up = remote(
        x.at[pl.ds(0, BLOCK)],
        stack.at[pl.ds(BLOCK + ROWS, BLOCK)],
        x_send.at[1],
        x_recv.at[1],
        (section, above),
    )
    c_down = remote(
        cot.at[pl.ds(ROWS - NARROW, NARROW)],
        stack_g.at[pl.ds(0, NARROW)],
        c_send.at[0],
        c_recv.at[0],
        (section, below),
    )
    c_up = remote(
        cot.at[pl.ds(0, NARROW)],
        stack_g.at[pl.ds(NARROW + ROWS, NARROW)],
        c_send.at[1],
        c_recv.at[1],
        (section, above),
    )
    x_down.start()
    x_up.start()

    @pl.when(section == 0)
    def _():
        c_down.start()
        c_up.start()

    stack[BLOCK : BLOCK + ROWS, :] = x[...]
    stack_g[NARROW : NARROW + ROWS, :] = cot[...]
    bias_rows = jnp.concatenate([bias[...]] * 4, axis=1)

    def hop(level, group, peer):
        part = (pl.ds(0, PLANS[level]["sent"]), pl.ds(group * GROUP, GROUP))
        return remote(g_out.at[part], g_in.at[part], g_send.at[group], g_recv.at[group], peer)

    def live_of(level, group):
        lane = iota((PLANS[level]["tall"], GROUP), 1)
        return lane + group * GROUP < PLANS[level]["cols"] * CH

    def conv_of(tall, ref, which, group_list):
        windows = [ref[0:tall, lanes(group * GROUP, 2 * GROUP)] for group in group_list]
        three = mat(jnp.concatenate(windows, axis=0), bands[which])
        result = []
        for index in range(len(group_list)):
            part = three[index * tall : (index + 1) * tall]
            result.append(
                pltpu.roll(part[:, :GROUP], 1, 0)
                + part[:, GROUP : 2 * GROUP]
                + pltpu.roll(part[:, 2 * GROUP :], tall - 1, 0)
            )
        return zip(group_list, result)

    def save_noise(level):
        plan = PLANS[level]
        rows, back, groups = plan["rows"], plan["back"], plan["groups"]
        shape = (ROWS, back)
        choose = one_hot(
            (iota(shape, 1) == iota(shape, 0) + plan["lead"]) & (iota(shape, 0) < rows)
        )

        def save(group_list):
            for group in group_list:
                span_lanes = lanes(group * GROUP, GROUP)
                noise[:, span_lanes] = mat(choose, back_b[0:back, span_lanes]).astype(
                    jnp.bfloat16
                )

        each_group(groups, save, plan["chunk"])
        if groups * GROUP < COLS * CH:
            noise[:, groups * GROUP :] = jnp.zeros(
                (ROWS, COLS * CH - groups * GROUP), jnp.bfloat16
            )

    def finish_last():
        level = SECTIONS - 1
        back = PLANS[level]["back"]

        def back_last(group_list):
            for group, value in conv_of(back, ei_b, 3, group_list):
                value = jnp.where(live_of(level, group)[:back], value, 0.0)
                back_b[0:back, lanes(group * GROUP, GROUP)] = value.astype(jnp.bfloat16)

        each_group(PLANS[level]["groups"], back_last, PLANS[level]["chunk"])
        save_noise(level)

    def run_section(level):
        plan = PLANS[level]
        rows, lead, tall = plan["rows"], plan["lead"], plan["tall"]
        groups, chunk, back = plan["groups"], plan["chunk"], plan["back"]
        image = iota((tall, GROUP), 0) - lead
        keep_rows = ((image >= 0) | (strip > 0)) & ((image < rows) | (strip < strips - 1))
        inner_rows = (image[:back] >= 0) & (image[:back] < rows)

        def live(group):
            return live_of(level, group)

        def live_back(group):
            return iota((back, GROUP), 1) + group * GROUP < plan["cols"] * CH

        def conv(ref, which, group_list):
            return conv_of(tall, ref, which, group_list)

        def conv_back(ref, which, group_list):
            return conv_of(back, ref, which, group_list)

        def put(ref, group, value):
            size = value.shape[0]
            ref[0:size, lanes(SIDE + group * GROUP, GROUP)] = value.astype(jnp.bfloat16)

        for ref in (x_b, h_b, eo_b, ei_b):
            zero = jnp.zeros((tall, SIDE), jnp.bfloat16)
            ref[0:tall, 0:SIDE] = zero
            ref[0:tall, SIDE + groups * GROUP : 2 * SIDE + groups * GROUP] = zero

        if level + 1 < SECTIONS:
            table = column_weights(level)
            across = iota((CH, SIDE), 1) - iota((CH, SIDE), 0)
            for group, start in enumerate(column_windows(level)):
                for fine in range(8):
                    for half in range(2):
                        coarse = 4 * group + 2 * half
                        low = table.get((start + fine, coarse), 0.0)
                        high = table.get((start + fine, coarse + 1), 0.0)
                        block = jnp.where(across == 0, low, 0.0) + jnp.where(
                            across == CH, high, 0.0
                        )
                        cols_m[
                            group,
                            CH * fine : CH * fine + CH,
                            SIDE * half : SIDE * half + SIDE,
                        ] = block.astype(jnp.bfloat16)

        x_down.wait_recv()
        x_up.wait_recv()
        span = 2 * BLOCK + ROWS
        at = iota((tall, span), 0) - lead
        slot = iota((tall, span), 1)
        want = jnp.where(
            at < 0,
            at + rows - plan["first"],
            jnp.where(at < rows, at + BLOCK, at - rows + BLOCK + ROWS),
        )
        near = (at >= -plan["halo"]) & (at < rows + plan["halo"])
        near = near & ((at >= 0) | (strip > 0)) & ((at < rows) | (strip < strips - 1))
        pick = one_hot((slot == want) & near)

        def load_x(group_list):
            for group in group_list:
                value = mat(pick, stack[:, lanes(group * GROUP, GROUP)])
                put(x_b, group, jnp.where(live(group), value, 0.0))

        each_group(groups, load_x, chunk)

        def forward_in(group_list):
            for group, value in conv(x_b, 0, group_list):
                value = value + bias_rows[0:1, :]
                soft = jnp.maximum(value, 0.0) + jnp.log(1.0 + jnp.exp(-jnp.abs(value)))
                hidden = LEAK * value + (1.0 - LEAK) * soft
                keep = keep_rows & live(group)
                put(h_b, group, jnp.where(keep, hidden, 0.0))
                slope = jnp.where(keep, steepness(value), 0.0)
                slope_in[0:tall, lanes(group * GROUP, GROUP)] = slope

        each_group(groups, forward_in, chunk)

        def forward_out(group_list):
            for group, value in conv(h_b, 1, group_list):
                value = value + bias_rows[1:2, :]
                slope = jnp.where(live(group), steepness(value), 0.0)
                slope_out[0:tall, lanes(group * GROUP, GROUP)] = slope

        each_group(groups, forward_out, chunk)

        if level == 0:
            c_down.wait_recv()
            c_up.wait_recv()
            span_g = 2 * NARROW + ROWS
            at_g = iota((back, span_g), 0) - lead
            near_g = ((at_g >= 0) | (strip > 0)) & ((at_g < rows) | (strip < strips - 1))
            pick_g = one_hot((iota((back, span_g), 1) == at_g + NARROW) & near_g)

            def load_g(group_list):
                for group in group_list:
                    span_lanes = lanes(group * GROUP, GROUP)
                    value = mat(pick_g, stack_g[:, span_lanes])
                    g_b[0:back, span_lanes] = value
                    put(eo_b, group, value * slope_out[0:back, span_lanes])

            each_group(groups, load_g, chunk)
        else:
            sent = min(plan["sent"], back)
            for group in range(groups):
                hop(level, group, (finer, strip)).wait_recv()
                span_lanes = lanes(group * GROUP, GROUP)
                value = g_in[0:sent, span_lanes].astype(jnp.float32)
                if sent < back:
                    rest = jnp.zeros((back - sent, GROUP), jnp.float32)
                    value = jnp.concatenate([value, rest], axis=0)
                g_b[0:back, span_lanes] = value
                put(eo_b, group, value * slope_out[0:back, span_lanes])

        def error_in(group_list):
            for group, value in conv_back(eo_b, 2, group_list):
                put(ei_b, group, value * slope_in[0:back, lanes(group * GROUP, GROUP)])

        each_group(groups, error_in, chunk)

        def back_input(group_list):
            for group, value in conv_back(ei_b, 3, group_list):
                span_lanes = lanes(group * GROUP, GROUP)
                value = jnp.where(live_back(group), value, 0.0)
                back_b[0:back, span_lanes] = value.astype(jnp.bfloat16)
                total = g_b[0:back, span_lanes] + value
                up_b[0:back, span_lanes] = total.astype(jnp.bfloat16)

        if level + 1 < SECTIONS:
            after = PLANS[level + 1]
            shape = (after["tall"], back)
            coarse_row = strip * after["rows"] + iota(shape, 0) - after["lead"]
            local_row = iota(shape, 1) - lead
            fine_row = strip * rows + local_row
            num = jnp.maximum(6 * fine_row - 1, 0)
            low = num >> 3
            frac = (num & 7).astype(jnp.float32) * 0.125
            high = jnp.minimum(low + 1, strips * after["rows"] - 1)
            real = (fine_row >= 0) & (fine_row < strips * rows)
            real = real & (local_row >= -plan["reach"]) & (local_row < rows + plan["reach"])
            real = real & (coarse_row >= 0) & (coarse_row < strips * after["rows"])
            row_m = jnp.where(coarse_row == low, 1.0 - frac, 0.0)
            row_m = row_m + jnp.where(coarse_row == high, frac, 0.0)
            row_m = jnp.where(real, row_m, 0.0).astype(jnp.bfloat16)

            windows = column_windows(level)
            ready = 0
            begin = 0
            for size in LAST_CHUNKS[level]:
                part = list(range(begin, begin + size))
                begin += size
                back_input(part)
                for group in part:
                    span_lanes = lanes(group * GROUP, GROUP)
                    value = mat(row_m, up_b[0:back, span_lanes])
                    row_b[0 : after["tall"], span_lanes] = value.astype(jnp.bfloat16)
                while ready < len(windows) and windows[ready] + 8 <= 4 * begin:
                    start = CH * windows[ready]
                    value = mat(
                        row_b[0 : after["tall"], start : start + 2 * GROUP], cols_m[ready]
                    )
                    g_out[0 : after["tall"], GROUP * ready : GROUP * ready + GROUP] = (
                        value.astype(jnp.bfloat16)
                    )
                    hop(level + 1, ready, (coarser, strip)).start()
                    ready += 1
            assert ready == len(windows)

        if level + 1 < SECTIONS:
            save_noise(level)

        for which, (field, error) in enumerate(((x_b, ei_b), (h_b, eo_b))):
            bias_acc[which : which + 1, :] = jnp.zeros((1, GROUP), jnp.float32)

            def pile(group_list):
                for group in group_list:
                    if isinstance(group, int):
                        where_rows = pl.ds(group * back, back)
                    else:
                        where_rows = pl.ds(pl.multiple_of(group * back, 16), back)
                    tall_x[where_rows, :] = field[0:back, lanes(group * GROUP, 2 * GROUP)]
                    value = error[0:back, lanes(SIDE + group * GROUP, GROUP)]
                    value = jnp.where(inner_rows, value.astype(jnp.float32), 0.0)
                    bias_acc[which : which + 1, :] += jnp.sum(value, axis=0, keepdims=True)
                    tall_e[where_rows, 0:GROUP] = pltpu.roll(value, back - 1, 0).astype(
                        jnp.bfloat16
                    )
                    tall_e[where_rows, GROUP : 2 * GROUP] = value.astype(jnp.bfloat16)
                    tall_e[where_rows, 2 * GROUP :] = pltpu.roll(value, 1, 0).astype(
                        jnp.bfloat16
                    )

            each_group(groups, pile, chunk)
            grid_a[which] = lax.dot_general(
                tall_x[0 : groups * back, :],
                tall_e[0 : groups * back, :],
                (((0,), (0,)), ((), ())),
                preferred_element_type=jnp.float32,
            )

    for level in range(SECTIONS):

        @pl.when(section == level)
        def _():
            run_section(level)

    def folded(which, tap):
        dy, dx = tap // 3, tap % 3
        low, high = 0.0, 0.0
        for half in range(2):
            span_lanes = slice(GROUP * dy + SIDE * half, GROUP * dy + SIDE * half + SIDE)
            row = CH * (2 * half + dx + 1)
            low = low + grid_a[which, row : row + CH, span_lanes]
            high = high + grid_a[which, row + CH : row + 2 * CH, span_lanes]
        return low, high

    left = iota((CH, SIDE), 1) < CH
    blocks = []
    for pair in range(9):
        low_a, high_a = folded((2 * pair) // 9, (2 * pair) % 9)
        low_b, high_b = folded((2 * pair + 1) // 9, (2 * pair + 1) % 9)
        blocks.append(
            jnp.where(left, low_a + pltpu.roll(high_a, CH, 1), high_b + pltpu.roll(low_b, CH, 1))
        )
    sums = bias_acc[:, 0:SIDE] + bias_acc[:, SIDE:]
    sums = sums + pltpu.roll(sums, CH, 1)
    tail = jnp.where(iota((8, SIDE), 1) < CH, sums[0:1, :], sums[1:2, :])
    blocks.append(jnp.where(iota((8, SIDE), 0) == 0, tail, 0.0))
    blocks.append(jnp.zeros((PIECES * PIECE - 9 * CH - 8, SIDE), jnp.float32))
    packed[...] = jnp.concatenate(blocks, axis=0).reshape(PIECES, PIECE, SIDE)

    scale = 0.0
    for level, plan in enumerate(PLANS):
        factor = 1.0 / math.sqrt(strips * plan["rows"] * plan["cols"])
        scale = jnp.where(section == level, jnp.float32(factor), scale)

    def meanwhile():
        @pl.when(section == SECTIONS - 1)
        def _():
            finish_last()

    strip_sum(
        lambda a, b, c, d, peer: remote(a, b, c, d, (section, peer)),
        strip,
        scale,
        meanwhile,
        packed,
        *sum_refs,
    )
    sums_out[...] = sum_refs[6][...]

    x_down.wait_send()
    x_up.wait_send()

    @pl.when(section == 0)
    def _():
        c_down.wait_send()
        c_up.wait_send()

    for level in range(1, SECTIONS):

        @pl.when(section == level - 1)
        def _():
            for group in range(PLANS[level]["groups"]):
                hop(level, group, (coarser, strip)).wait_send()


def chain(x, cot, taps, bias):
    dma = pltpu.SemaphoreType.DMA
    half, full = jnp.bfloat16, jnp.float32
    padded = WIDE + 2 * SIDE
    in_vmem = pl.BlockSpec(memory_space=pltpu.VMEM)
    return pl.pallas_call(
        chain_body,
        out_shape=(
            jax.ShapeDtypeStruct((ROWS, COLS * CH), half),
            jax.ShapeDtypeStruct((PIECES, PIECE, SIDE), half),
        ),
        in_specs=[in_vmem] * 4,
        out_specs=(in_vmem, in_vmem),
        scratch_shapes=[
            pltpu.VMEM((2 * BLOCK + ROWS, COLS * CH), half),
            pltpu.VMEM((2 * NARROW + ROWS, COLS * CH), half),
            pltpu.VMEM((4, 2 * GROUP, 3 * GROUP), half),
            pltpu.VMEM((TALL, padded), half),
            pltpu.VMEM((TALL, padded), half),
            pltpu.VMEM((TALL, padded), half),
            pltpu.VMEM((TALL, padded), half),
            pltpu.VMEM((TALL, WIDE), full),
            pltpu.VMEM((TALL, WIDE), full),
            pltpu.VMEM((TALL, WIDE), full),
            pltpu.VMEM((TALL, WIDE), half),
            pltpu.VMEM((TALL, WIDE), half),
            pltpu.VMEM((NEXT_TALL, WIDE), half),
            pltpu.VMEM((NEXT_TALL, NEXT_WIDE), half),
            pltpu.VMEM((NEXT_TALL, NEXT_WIDE), half),
            pltpu.VMEM((NEXT_WIDE // GROUP, 2 * GROUP, GROUP), half),
            pltpu.VMEM((DEEP, 2 * GROUP), half),
            pltpu.VMEM((DEEP, 3 * GROUP), half),
            pltpu.VMEM((2, 2 * GROUP, 3 * GROUP), full),
            pltpu.VMEM((2, GROUP), full),
            pltpu.VMEM((PIECES, PIECE, SIDE), full),
            dma((2,)), dma((2,)), dma((2,)), dma((2,)),
            dma((NEXT_WIDE // GROUP,)), dma((NEXT_WIDE // GROUP,)),
            pltpu.VMEM((RING, PIECE, SIDE), full),
            pltpu.VMEM((RING, PIECE, SIDE), full),
            pltpu.VMEM((RING, PIECE, SIDE), half),
            pltpu.VMEM((RING - 1, PIECE, SIDE), half),
            pltpu.VMEM((PIECE, SIDE), half),
            pltpu.VMEM((RING, PIECE, SIDE), half),
            pltpu.VMEM((PIECES, PIECE, SIDE), half),
            dma, dma,
            dma((RING - 1,)), dma((RING - 1,)),
            dma((RING - 1,)), dma((RING - 1,)),
            dma((RING - 1,)), dma((RING - 1,)),
            dma((RING,)), dma((RING,)),
        ],
        compiler_params=pltpu.CompilerParams(
            collective_id=0, has_side_effects=True, vmem_limit_bytes=48 << 20
        ),
    )(x, cot, taps, bias)


def write_body(noise_in, sums_in, noise, kernel_out, bias_out, final):
    noise[...] = noise_in[...]
    final[...] = sums_in[...].astype(jnp.float32).reshape(PIECES * PIECE, SIDE)
    for pair in range(9):
        block = final[CH * pair : CH * pair + CH, :]
        kernel_out[2 * pair] = block[:, :CH]
        kernel_out[2 * pair + 1] = pltpu.roll(block, CH, 1)[:, :CH]
    sums = final[9 * CH : 9 * CH + 8, :]
    bias_out[0:1, :] = sums[0:1, :CH]
    bias_out[1:2, :] = pltpu.roll(sums, CH, 1)[0:1, :CH]


def write_out(noise, sums):
    in_vmem = pl.BlockSpec(memory_space=pltpu.VMEM)
    full = jnp.float32
    return pl.pallas_call(
        write_body,
        out_shape=(
            jax.ShapeDtypeStruct(noise.shape, noise.dtype),
            jax.ShapeDtypeStruct((18, CH, CH), full),
            jax.ShapeDtypeStruct((2, CH), full),
        ),
        in_specs=[in_vmem] * 2,
        out_specs=(in_vmem,) * 3,
        scratch_shapes=[pltpu.VMEM((PIECES * PIECE, SIDE), full)],
        compiler_params=pltpu.CompilerParams(vmem_limit_bytes=8 << 20),
    )(noise, sums)


def local(cotangent, activations, weights, biases):
    taps = weights.reshape(2, 9, CH, CH)
    noise, sums = chain(activations[0, 0], cotangent[0], taps, biases[0])
    noise, kernels, sums = write_out(noise, sums)
    return (
        noise[None, None],
        kernels.reshape(1, 2, 3, 3, CH, CH),
        sums[None],
    )


def solution(mesh):
    return jax.shard_map(
        local,
        mesh=mesh,
        in_specs=(
            P(None, "strip", None),
            P("section", None, "strip", None),
            P("section", None, None, None, None, None),
            P("section", None, None),
        ),
        out_specs=(
            P("section", None, "strip", None),
            P("section", None, None, None, None, None),
            P("section", None, None),
        ),
        check_vma=False,
    )
```

```python
import math

import jax
import jax.numpy as jnp
from jax import lax
from jax.experimental import pallas as pl
from jax.experimental.pallas import tpu as pltpu
from jax.sharding import PartitionSpec as P

LEAK = 0.05
RING = 8
PIECE = 40
PIECES = 2 * RING
MESH = pl.DeviceIdType.MESH


def sum_peers(strip):
    core = lax.rem(strip, 2)
    row = lax.rem(lax.div(strip, 2), RING)
    deep = lax.div(strip, 2 * RING)
    partner = strip + 1 - 2 * core
    along_y = [(deep * RING + lax.rem(row + step, RING)) * 2 + core for step in range(1, RING)]
    along_z = [(lax.rem(deep + step, RING) * RING + row) * 2 + core for step in range(1, RING)]
    return core, row, deep, partner, along_y, along_z


def strip_sum(
    remote, strip, scale, meanwhile, src, pair_in, y_sum, y_out, y_in, z_out, z_in, gathered,
    pair_send, pair_recv, y_send, y_recv, z_send, z_recv, g_send, g_recv, p_send, p_recv,
):
    core, row, deep, partner, along_y, along_z = sum_peers(strip)
    mine = core * RING
    swap = remote(
        src.at[pl.ds((1 - core) * RING, RING)], pair_in, pair_send, pair_recv, partner
    )
    swap.start()
    swap.wait()
    both = src[pl.ds(mine, RING)] + pair_in[...]
    y_sum[...] = both
    y_out[...] = both.astype(jnp.bfloat16)
    scatter = []
    for step in range(1, RING):
        copy = remote(
            y_out.at[lax.rem(row + step, RING)],
            y_in.at[step - 1],
            y_send.at[step - 1],
            y_recv.at[step - 1],
            along_y[step - 1],
        )
        copy.start()
        scatter.append(copy)
    meanwhile()
    total = y_sum[row]
    for step in range(1, RING):
        scatter[step - 1].wait_recv()
        total = total + y_in[step - 1].astype(jnp.float32)
    z_out[...] = total.astype(jnp.bfloat16)
    z_in[deep] = total.astype(jnp.bfloat16)
    trade = []
    for step in range(1, RING):
        copy = remote(
            z_out, z_in.at[deep], z_send.at[step - 1], z_recv.at[step - 1], along_z[step - 1]
        )
        copy.start()
        trade.append(copy)
    for copy in trade:
        copy.wait_recv()
    total = z_in[0].astype(jnp.float32)
    for index in range(1, RING):
        total = total + z_in[index].astype(jnp.float32)
    own = mine + row
    gathered[own] = (total * scale).astype(jnp.bfloat16)
    gather = []
    for step in range(1, RING):
        copy = remote(
            gathered.at[own],
            gathered.at[own],
            g_send.at[step - 1],
            g_recv.at[step - 1],
            along_y[step - 1],
        )
        copy.start()
        gather.append(copy)
    passed = [
        remote(gathered.at[own], gathered.at[own], p_send.at[0], p_recv.at[0], partner)
    ]
    passed[0].start()
    for step in range(1, RING):
        gather[step - 1].wait_recv()
        came = mine + lax.rem(row + RING - step, RING)
        copy = remote(
            gathered.at[came], gathered.at[came], p_send.at[step], p_recv.at[step], partner
        )
        copy.start()
        passed.append(copy)
    for copy in passed:
        copy.wait_recv()
    for copy in scatter + trade + gather + passed:
        copy.wait_send()


SECTIONS = 4
ROWS = 64
COLS = 32
CH = 64
GROUP = 4 * CH
SIDE = 2 * CH
BLOCK = 32
NARROW = 16
CHUNKS = (4, 3, 5, 4)
WAIT, INNER, OUTER = range(3)
STEPS = (
    ((INNER, 0, 4), (OUTER, 0, 3), (INNER, 4, 8), (OUTER, 3, 6), (OUTER, 6, 8)),
    ((WAIT, 0, 4), (INNER, 0, 3), (OUTER, 0, 2), (WAIT, 4, 6), (INNER, 3, 6), (OUTER, 2, 6)),
    ((WAIT, 0, 5), (INNER, 0, 5), (OUTER, 0, 5)),
    ((WAIT, 0, 4), (INNER, 0, 4)),
)


def plans():
    reach = [0] * SECTIONS
    for level in reversed(range(SECTIONS - 1)):
        reach[level] = (8 * (reach[level + 1] + 2) + 7) // 6
    result = []
    for level in range(SECTIONS):
        rows = ROWS * 3**level // 4**level
        cols = COLS * 3**level // 4**level
        halo = reach[level] + 4
        lead = halo
        tall = -(-(lead + rows + halo) // 16) * 16
        first = max(0, (rows - halo) // 16 * 16)
        first = min(first, ROWS - BLOCK)
        if rows - first > BLOCK:
            first += 16
        result.append(
            dict(
                rows=rows,
                cols=cols,
                reach=reach[level],
                halo=halo,
                lead=lead,
                tall=tall,
                groups=-(-cols // 4),
                first=first,
                sent=-(-(lead + rows + reach[level] + 2) // 8) * 8,
                chunk=CHUNKS[level],
                back=-(-(rows + 2 * halo - 2) // 16) * 16,
            )
        )
    return result


PLANS = plans()
TALL = max(plan["tall"] for plan in PLANS)
WIDE = max(plan["groups"] for plan in PLANS) * GROUP
NEXT_TALL = max(plan["tall"] for plan in PLANS[1:])
NEXT_WIDE = max(plan["groups"] for plan in PLANS[1:]) * GROUP
DEEP = max(plan["back"] * plan["groups"] for plan in PLANS)


def column_weights(level):
    fine, coarse = PLANS[level]["cols"], PLANS[level + 1]["cols"]
    table = {}
    for col in range(fine):
        num = max((2 * col + 1) * coarse - fine, 0)
        low = num // (2 * fine)
        frac = (num - 2 * fine * low) / (2 * fine)
        high = min(low + 1, coarse - 1)
        table[col, low] = table.get((col, low), 0.0) + 1.0 - frac
        table[col, high] = table.get((col, high), 0.0) + frac
    return {key: value for key, value in table.items() if value != 0.0}


def column_windows(level):
    table = column_weights(level)
    limit = PLANS[level]["groups"] * 4 - 8
    starts = []
    for group in range(PLANS[level + 1]["groups"]):
        used = [fine for fine, coarse in table if coarse // 4 == group]
        start = min(min(used) // 2 * 2, limit)
        assert max(used) < start + 8
        starts.append(start)
    return starts


def iota(shape, axis):
    return lax.broadcasted_iota(jnp.int32, shape, axis)


def mat(left, right):
    return jnp.dot(left, right, preferred_element_type=jnp.float32)


def steepness(value):
    half = 0.5 * (1.0 - LEAK)
    return (LEAK + half) + half * jnp.tanh(0.5 * value)


def one_hot(cond):
    return jnp.where(cond, 1.0, 0.0).astype(jnp.bfloat16)


def each_group(count, body, step):
    def run(index, carry):
        body([index * step + extra for extra in range(step)])
        return carry

    if step == count:
        body(list(range(count)))
    else:
        lax.fori_loop(0, count // step, run, 0)


def lanes(start, size):
    if isinstance(start, int):
        return pl.ds(start, size)
    return pl.ds(pl.multiple_of(start, 128), size)


def chain_body(
    x, cot, taps, bias, noise, sums_out,
    stack, stack_g, bands, x_b, h_b, eo_b, ei_b, slope_in, slope_out, g_b, back_b, up_b,
    row_b, g_out, g_in, cols_m, tall_x, tall_e, grid_a, bias_acc,
    packed, taps_v, bias_v, local_sem, x_send, x_recv, c_send, c_recv, g_send, g_recv, *sum_refs,
):
    section = lax.axis_index("section")
    strip = lax.axis_index("strip")
    strips = lax.axis_size("strip")
    below = lax.rem(strip + 1, strips)
    above = lax.rem(strip + strips - 1, strips)
    coarser = lax.rem(section + 1, SECTIONS)
    finer = lax.rem(section + SECTIONS - 1, SECTIONS)

    fetches = [
        pltpu.make_async_copy(taps, taps_v, local_sem.at[0]),
        pltpu.make_async_copy(bias, bias_v, local_sem.at[1]),
        pltpu.make_async_copy(x, stack.at[pl.ds(BLOCK, ROWS)], local_sem.at[2]),
        pltpu.make_async_copy(cot, stack_g.at[pl.ds(NARROW, ROWS)], local_sem.at[3]),
    ]
    for fetch in fetches:
        fetch.start()
    barrier = pltpu.get_barrier_semaphore()
    partner, along_y, along_z = sum_peers(strip)[3:]
    peers = [(section, below), (section, above), (coarser, strip), (finer, strip)]
    peers += [(section, peer) for peer in [partner] + along_y + along_z]
    for peer in peers:
        pl.semaphore_signal(barrier, inc=1, device_id=peer, device_id_type=MESH)

    bands[...] = jnp.zeros_like(bands)
    fetches[0].wait()
    blank = jnp.zeros((CH, CH), jnp.float32)
    for which, (source, flip) in enumerate(((0, False), (1, False), (1, True), (0, True))):
        for dy in range(3):
            tap_list = []
            for dx in range(3):
                at = (2 - dy) * 3 + 2 - dx if flip else dy * 3 + dx
                tap_list.append(taps_v[source, at].astype(jnp.float32))
            tap_list.append(blank)
            for index in range(4):
                pair = (tap_list[index], tap_list[index - 1])
                if flip:
                    block = jnp.concatenate(pair, axis=0).T
                else:
                    block = jnp.concatenate(pair, axis=1)
                block = block.astype(jnp.bfloat16)
                for half in range(2):
                    row = CH * (2 * half + 1 + index)
                    col = GROUP * dy + SIDE * half
                    bands[which, row : row + CH, col : col + SIDE] = block

    pl.semaphore_wait(barrier, len(peers))

    def remote(src_ref, dst_ref, send, recv, peer):
        return pltpu.make_async_remote_copy(
            src_ref=src_ref,
            dst_ref=dst_ref,
            send_sem=send,
            recv_sem=recv,
            device_id=peer,
            device_id_type=MESH,
        )

    first = PLANS[0]["first"]
    for level in range(1, SECTIONS):
        first = jnp.where(section >= level, PLANS[level]["first"], first)
    x_down = remote(
        x.at[pl.ds(pl.multiple_of(first, 16), BLOCK)],
        stack.at[pl.ds(0, BLOCK)],
        x_send.at[0],
        x_recv.at[0],
        (section, below),
    )
    x_up = remote(
        x.at[pl.ds(0, BLOCK)],
        stack.at[pl.ds(BLOCK + ROWS, BLOCK)],
        x_send.at[1],
        x_recv.at[1],
        (section, above),
    )
    c_down = remote(
        cot.at[pl.ds(ROWS - NARROW, NARROW)],
        stack_g.at[pl.ds(0, NARROW)],
        c_send.at[0],
        c_recv.at[0],
        (section, below),
    )
    c_up = remote(
        cot.at[pl.ds(0, NARROW)],
        stack_g.at[pl.ds(NARROW + ROWS, NARROW)],
        c_send.at[1],
        c_recv.at[1],
        (section, above),
    )
    x_down.start()
    x_up.start()

    @pl.when(section == 0)
    def _():
        c_down.start()
        c_up.start()

    for fetch in fetches[1:]:
        fetch.wait()
    bias_rows = jnp.concatenate([bias_v[...]] * 4, axis=1)

    def hop(level, group, peer):
        part = (pl.ds(0, PLANS[level]["sent"]), pl.ds(group * GROUP, GROUP))
        return remote(g_out.at[part], g_in.at[part], g_send.at[group], g_recv.at[group], peer)

    def live_of(level, group):
        lane = iota((PLANS[level]["tall"], GROUP), 1)
        return lane + group * GROUP < PLANS[level]["cols"] * CH

    def conv_of(tall, ref, which, group_list):
        windows = [ref[0:tall, lanes(group * GROUP, 2 * GROUP)] for group in group_list]
        three = mat(jnp.concatenate(windows, axis=0), bands[which])
        result = []
        for index in range(len(group_list)):
            part = three[index * tall : (index + 1) * tall]
            result.append(
                pltpu.roll(part[:, :GROUP], 1, 0)
                + part[:, GROUP : 2 * GROUP]
                + pltpu.roll(part[:, 2 * GROUP :], tall - 1, 0)
            )
        return zip(group_list, result)

    def save_noise(level):
        plan = PLANS[level]
        rows, back, groups = plan["rows"], plan["back"], plan["groups"]
        shape = (ROWS, back)
        choose = one_hot(
            (iota(shape, 1) == iota(shape, 0) + plan["lead"]) & (iota(shape, 0) < rows)
        )

        def save(group_list):
            for group in group_list:
                span_lanes = lanes(group * GROUP, GROUP)
                noise[:, span_lanes] = mat(choose, back_b[0:back, span_lanes]).astype(
                    jnp.bfloat16
                )

        each_group(groups, save, plan["chunk"])
        if groups * GROUP < COLS * CH:
            noise[:, groups * GROUP :] = jnp.zeros(
                (ROWS, COLS * CH - groups * GROUP), jnp.bfloat16
            )

    def finish_last():
        level = SECTIONS - 1
        back = PLANS[level]["back"]

        def back_last(group_list):
            for group, value in conv_of(back, ei_b, 3, group_list):
                value = jnp.where(live_of(level, group)[:back], value, 0.0)
                back_b[0:back, lanes(group * GROUP, GROUP)] = value.astype(jnp.bfloat16)

        each_group(PLANS[level]["groups"], back_last, PLANS[level]["chunk"])
        save_noise(level)

    def run_section(level):
        plan = PLANS[level]
        rows, lead, tall = plan["rows"], plan["lead"], plan["tall"]
        groups, chunk, back = plan["groups"], plan["chunk"], plan["back"]
        image = iota((tall, GROUP), 0) - lead
        keep_rows = ((image >= 0) | (strip > 0)) & ((image < rows) | (strip < strips - 1))
        inner_rows = (image[:back] >= 0) & (image[:back] < rows)

        def live(group):
            return live_of(level, group)

        def live_back(group):
            return iota((back, GROUP), 1) + group * GROUP < plan["cols"] * CH

        def conv(ref, which, group_list):
            return conv_of(tall, ref, which, group_list)

        def conv_back(ref, which, group_list):
            return conv_of(back, ref, which, group_list)

        def put(ref, group, value):
            size = value.shape[0]
            ref[0:size, lanes(SIDE + group * GROUP, GROUP)] = value.astype(jnp.bfloat16)

        for ref in (x_b, h_b, eo_b, ei_b):
            zero = jnp.zeros((tall, SIDE), jnp.bfloat16)
            ref[0:tall, 0:SIDE] = zero
            ref[0:tall, SIDE + groups * GROUP : 2 * SIDE + groups * GROUP] = zero

        if level + 1 < SECTIONS:
            table = column_weights(level)
            across = iota((CH, SIDE), 1) - iota((CH, SIDE), 0)
            for group, start in enumerate(column_windows(level)):
                for fine in range(8):
                    for half in range(2):
                        coarse = 4 * group + 2 * half
                        low = table.get((start + fine, coarse), 0.0)
                        high = table.get((start + fine, coarse + 1), 0.0)
                        block = jnp.where(across == 0, low, 0.0) + jnp.where(
                            across == CH, high, 0.0
                        )
                        cols_m[
                            group,
                            CH * fine : CH * fine + CH,
                            SIDE * half : SIDE * half + SIDE,
                        ] = block.astype(jnp.bfloat16)

        x_down.wait_recv()
        x_up.wait_recv()
        span = 2 * BLOCK + ROWS
        at = iota((tall, span), 0) - lead
        slot = iota((tall, span), 1)
        want = jnp.where(
            at < 0,
            at + rows - plan["first"],
            jnp.where(at < rows, at + BLOCK, at - rows + BLOCK + ROWS),
        )
        near = (at >= -plan["halo"]) & (at < rows + plan["halo"])
        near = near & ((at >= 0) | (strip > 0)) & ((at < rows) | (strip < strips - 1))
        pick = one_hot((slot == want) & near)

        def load_x(group_list):
            for group in group_list:
                value = mat(pick, stack[:, lanes(group * GROUP, GROUP)])
                put(x_b, group, jnp.where(live(group), value, 0.0))

        each_group(groups, load_x, chunk)

        def forward_in(group_list):
            for group, value in conv(x_b, 0, group_list):
                value = value + bias_rows[0:1, :]
                soft = jnp.maximum(value, 0.0) + jnp.log(1.0 + jnp.exp(-jnp.abs(value)))
                hidden = LEAK * value + (1.0 - LEAK) * soft
                keep = keep_rows & live(group)
                put(h_b, group, jnp.where(keep, hidden, 0.0))
                slope = jnp.where(keep, steepness(value), 0.0)
                slope_in[0:tall, lanes(group * GROUP, GROUP)] = slope

        each_group(groups, forward_in, chunk)

        def forward_out(group_list):
            for group, value in conv(h_b, 1, group_list):
                value = value + bias_rows[1:2, :]
                slope = jnp.where(live(group), steepness(value), 0.0)
                slope_out[0:tall, lanes(group * GROUP, GROUP)] = slope

        each_group(groups, forward_out, chunk)

        if level == 0:
            c_down.wait_recv()
            c_up.wait_recv()
            span_g = 2 * NARROW + ROWS
            at_g = iota((back, span_g), 0) - lead
            near_g = ((at_g >= 0) | (strip > 0)) & ((at_g < rows) | (strip < strips - 1))
            pick_g = one_hot((iota((back, span_g), 1) == at_g + NARROW) & near_g)

            def load_g(group_list):
                for group in group_list:
                    span_lanes = lanes(group * GROUP, GROUP)
                    value = mat(pick_g, stack_g[:, span_lanes])
                    g_b[0:back, span_lanes] = value
                    put(eo_b, group, value * slope_out[0:back, span_lanes])

            each_group(groups, load_g, chunk)
        else:
            sent = min(plan["sent"], back)

            def arrive(group_list):
                for group in group_list:
                    hop(level, group, (finer, strip)).wait_recv()
                    span_lanes = lanes(group * GROUP, GROUP)
                    value = g_in[0:sent, span_lanes].astype(jnp.float32)
                    if sent < back:
                        rest = jnp.zeros((back - sent, GROUP), jnp.float32)
                        value = jnp.concatenate([value, rest], axis=0)
                    g_b[0:back, span_lanes] = value
                    put(eo_b, group, value * slope_out[0:back, span_lanes])

        def error_in(group_list):
            for group, value in conv_back(eo_b, 2, group_list):
                put(ei_b, group, value * slope_in[0:back, lanes(group * GROUP, GROUP)])

        def back_input(group_list):
            for group, value in conv_back(ei_b, 3, group_list):
                span_lanes = lanes(group * GROUP, GROUP)
                value = jnp.where(live_back(group), value, 0.0)
                back_b[0:back, span_lanes] = value.astype(jnp.bfloat16)
                total = g_b[0:back, span_lanes] + value
                up_b[0:back, span_lanes] = total.astype(jnp.bfloat16)

        if level + 1 < SECTIONS:
            after = PLANS[level + 1]
            shape = (after["tall"], back)
            coarse_row = strip * after["rows"] + iota(shape, 0) - after["lead"]
            local_row = iota(shape, 1) - lead
            fine_row = strip * rows + local_row
            num = jnp.maximum(6 * fine_row - 1, 0)
            low = num >> 3
            frac = (num & 7).astype(jnp.float32) * 0.125
            high = jnp.minimum(low + 1, strips * after["rows"] - 1)
            real = (fine_row >= 0) & (fine_row < strips * rows)
            real = real & (local_row >= -plan["reach"]) & (local_row < rows + plan["reach"])
            real = real & (coarse_row >= 0) & (coarse_row < strips * after["rows"])
            row_m = jnp.where(coarse_row == low, 1.0 - frac, 0.0)
            row_m = row_m + jnp.where(coarse_row == high, frac, 0.0)
            row_m = jnp.where(real, row_m, 0.0).astype(jnp.bfloat16)

            windows = column_windows(level)

        ready = 0
        for kind, begin, end in STEPS[level]:
            part = list(range(begin, end))
            if kind == WAIT:
                arrive(part)
            elif kind == INNER:
                error_in(part)
            else:
                back_input(part)
                for group in part:
                    span_lanes = lanes(group * GROUP, GROUP)
                    value = mat(row_m, up_b[0:back, span_lanes])
                    row_b[0 : after["tall"], span_lanes] = value.astype(jnp.bfloat16)
                while ready < len(windows) and windows[ready] + 8 <= 4 * end:
                    start = CH * windows[ready]
                    value = mat(
                        row_b[0 : after["tall"], start : start + 2 * GROUP], cols_m[ready]
                    )
                    g_out[0 : after["tall"], GROUP * ready : GROUP * ready + GROUP] = (
                        value.astype(jnp.bfloat16)
                    )
                    hop(level + 1, ready, (coarser, strip)).start()
                    ready += 1

        if level + 1 < SECTIONS:
            save_noise(level)

        for which, (field, error) in enumerate(((x_b, ei_b), (h_b, eo_b))):
            bias_acc[which : which + 1, :] = jnp.zeros((1, GROUP), jnp.float32)

            def pile(group_list):
                for group in group_list:
                    if isinstance(group, int):
                        where_rows = pl.ds(group * back, back)
                    else:
                        where_rows = pl.ds(pl.multiple_of(group * back, 16), back)
                    tall_x[where_rows, :] = field[0:back, lanes(group * GROUP, 2 * GROUP)]
                    value = error[0:back, lanes(SIDE + group * GROUP, GROUP)]
                    value = jnp.where(inner_rows, value.astype(jnp.float32), 0.0)
                    bias_acc[which : which + 1, :] += jnp.sum(value, axis=0, keepdims=True)
                    tall_e[where_rows, 0:GROUP] = pltpu.roll(value, back - 1, 0).astype(
                        jnp.bfloat16
                    )
                    tall_e[where_rows, GROUP : 2 * GROUP] = value.astype(jnp.bfloat16)
                    tall_e[where_rows, 2 * GROUP :] = pltpu.roll(value, 1, 0).astype(
                        jnp.bfloat16
                    )

            each_group(groups, pile, chunk)
            grid_a[which] = lax.dot_general(
                tall_x[0 : groups * back, :],
                tall_e[0 : groups * back, :],
                (((0,), (0,)), ((), ())),
                preferred_element_type=jnp.float32,
            )

    for level in range(SECTIONS):

        @pl.when(section == level)
        def _():
            run_section(level)

    def folded(which, tap):
        dy, dx = tap // 3, tap % 3
        low, high = 0.0, 0.0
        for half in range(2):
            span_lanes = slice(GROUP * dy + SIDE * half, GROUP * dy + SIDE * half + SIDE)
            row = CH * (2 * half + dx + 1)
            low = low + grid_a[which, row : row + CH, span_lanes]
            high = high + grid_a[which, row + CH : row + 2 * CH, span_lanes]
        return low, high

    left = iota((CH, SIDE), 1) < CH
    blocks = []
    for pair in range(9):
        low_a, high_a = folded((2 * pair) // 9, (2 * pair) % 9)
        low_b, high_b = folded((2 * pair + 1) // 9, (2 * pair + 1) % 9)
        blocks.append(
            jnp.where(left, low_a + pltpu.roll(high_a, CH, 1), high_b + pltpu.roll(low_b, CH, 1))
        )
    sums = bias_acc[:, 0:SIDE] + bias_acc[:, SIDE:]
    sums = sums + pltpu.roll(sums, CH, 1)
    tail = jnp.where(iota((8, SIDE), 1) < CH, sums[0:1, :], sums[1:2, :])
    blocks.append(jnp.where(iota((8, SIDE), 0) == 0, tail, 0.0))
    blocks.append(jnp.zeros((PIECES * PIECE - 9 * CH - 8, SIDE), jnp.float32))
    packed[...] = jnp.concatenate(blocks, axis=0).reshape(PIECES, PIECE, SIDE)

    scale = 0.0
    for level, plan in enumerate(PLANS):
        factor = 1.0 / math.sqrt(strips * plan["rows"] * plan["cols"])
        scale = jnp.where(section == level, jnp.float32(factor), scale)

    def meanwhile():
        @pl.when(section == SECTIONS - 1)
        def _():
            finish_last()

    strip_sum(
        lambda a, b, c, d, peer: remote(a, b, c, d, (section, peer)),
        strip,
        scale,
        meanwhile,
        packed,
        *sum_refs,
    )
    sums_out[...] = sum_refs[6][...]

    x_down.wait_send()
    x_up.wait_send()

    @pl.when(section == 0)
    def _():
        c_down.wait_send()
        c_up.wait_send()

    for level in range(1, SECTIONS):

        @pl.when(section == level - 1)
        def _():
            for group in range(PLANS[level]["groups"]):
                hop(level, group, (coarser, strip)).wait_send()


def chain(x, cot, taps, bias):
    dma = pltpu.SemaphoreType.DMA
    half, full = jnp.bfloat16, jnp.float32
    padded = WIDE + 2 * SIDE
    in_vmem = pl.BlockSpec(memory_space=pltpu.VMEM)
    return pl.pallas_call(
        chain_body,
        out_shape=(
            jax.ShapeDtypeStruct((ROWS, COLS * CH), half),
            jax.ShapeDtypeStruct((PIECES, PIECE, SIDE), half),
        ),
        in_specs=[pl.BlockSpec(memory_space=pltpu.HBM)] * 4,
        out_specs=(in_vmem, in_vmem),
        scratch_shapes=[
            pltpu.VMEM((2 * BLOCK + ROWS, COLS * CH), half),
            pltpu.VMEM((2 * NARROW + ROWS, COLS * CH), half),
            pltpu.VMEM((4, 2 * GROUP, 3 * GROUP), half),
            pltpu.VMEM((TALL, padded), half),
            pltpu.VMEM((TALL, padded), half),
            pltpu.VMEM((TALL, padded), half),
            pltpu.VMEM((TALL, padded), half),
            pltpu.VMEM((TALL, WIDE), full),
            pltpu.VMEM((TALL, WIDE), full),
            pltpu.VMEM((TALL, WIDE), full),
            pltpu.VMEM((TALL, WIDE), half),
            pltpu.VMEM((TALL, WIDE), half),
            pltpu.VMEM((NEXT_TALL, WIDE), half),
            pltpu.VMEM((NEXT_TALL, NEXT_WIDE), half),
            pltpu.VMEM((NEXT_TALL, NEXT_WIDE), half),
            pltpu.VMEM((NEXT_WIDE // GROUP, 2 * GROUP, GROUP), half),
            pltpu.VMEM((DEEP, 2 * GROUP), half),
            pltpu.VMEM((DEEP, 3 * GROUP), half),
            pltpu.VMEM((2, 2 * GROUP, 3 * GROUP), full),
            pltpu.VMEM((2, GROUP), full),
            pltpu.VMEM((PIECES, PIECE, SIDE), full),
            pltpu.VMEM((2, 9, CH, CH), half),
            pltpu.VMEM((2, CH), full),
            dma((4,)),
            dma((2,)), dma((2,)), dma((2,)), dma((2,)),
            dma((NEXT_WIDE // GROUP,)), dma((NEXT_WIDE // GROUP,)),
            pltpu.VMEM((RING, PIECE, SIDE), full),
            pltpu.VMEM((RING, PIECE, SIDE), full),
            pltpu.VMEM((RING, PIECE, SIDE), half),
            pltpu.VMEM((RING - 1, PIECE, SIDE), half),
            pltpu.VMEM((PIECE, SIDE), half),
            pltpu.VMEM((RING, PIECE, SIDE), half),
            pltpu.VMEM((PIECES, PIECE, SIDE), half),
            dma, dma,
            dma((RING - 1,)), dma((RING - 1,)),
            dma((RING - 1,)), dma((RING - 1,)),
            dma((RING - 1,)), dma((RING - 1,)),
            dma((RING,)), dma((RING,)),
        ],
        compiler_params=pltpu.CompilerParams(
            collective_id=0, has_side_effects=True, vmem_limit_bytes=67043328
        ),
    )(x, cot, taps, bias)


def write_body(noise_in, sums_in, noise, kernel_out, bias_out, final):
    noise[...] = noise_in[...]
    final[...] = sums_in[...].astype(jnp.float32).reshape(PIECES * PIECE, SIDE)
    for pair in range(9):
        block = final[CH * pair : CH * pair + CH, :]
        kernel_out[2 * pair] = block[:, :CH]
        kernel_out[2 * pair + 1] = pltpu.roll(block, CH, 1)[:, :CH]
    sums = final[9 * CH : 9 * CH + 8, :]
    bias_out[0:1, :] = sums[0:1, :CH]
    bias_out[1:2, :] = pltpu.roll(sums, CH, 1)[0:1, :CH]


def write_out(noise, sums):
    in_vmem = pl.BlockSpec(memory_space=pltpu.VMEM)
    full = jnp.float32
    return pl.pallas_call(
        write_body,
        out_shape=(
            jax.ShapeDtypeStruct(noise.shape, noise.dtype),
            jax.ShapeDtypeStruct((18, CH, CH), full),
            jax.ShapeDtypeStruct((2, CH), full),
        ),
        in_specs=[in_vmem] * 2,
        out_specs=(in_vmem,) * 3,
        scratch_shapes=[pltpu.VMEM((PIECES * PIECE, SIDE), full)],
        compiler_params=pltpu.CompilerParams(vmem_limit_bytes=67043328),
    )(noise, sums)


def local(cotangent, activations, weights, biases):
    taps = weights.reshape(2, 9, CH, CH)
    noise, sums = chain(activations[0, 0], cotangent[0], taps, biases[0])
    noise, kernels, sums = write_out(noise, sums)
    return (
        noise[None, None],
        kernels.reshape(1, 2, 3, 3, CH, CH),
        sums[None],
    )


def solution(mesh):
    return jax.shard_map(
        local,
        mesh=mesh,
        in_specs=(
            P(None, "strip", None),
            P("section", None, "strip", None),
            P("section", None, None, None, None, None),
            P("section", None, None),
        ),
        out_specs=(
            P("section", None, "strip", None),
            P("section", None, None, None, None, None),
            P("section", None, None),
        ),
        check_vma=False,
    )
```

```python
import math

import jax
import jax.numpy as jnp
from jax import lax
from jax.experimental import pallas as pl
from jax.experimental.pallas import tpu as pltpu
from jax.sharding import PartitionSpec as P

LEAK = 0.05
RING = 8
PIECE = 40
PIECES = 2 * RING
MESH = pl.DeviceIdType.MESH


def sum_peers(strip):
    core = lax.rem(strip, 2)
    row = lax.rem(lax.div(strip, 2), RING)
    deep = lax.div(strip, 2 * RING)
    partner = strip + 1 - 2 * core
    along_y = [(deep * RING + lax.rem(row + step, RING)) * 2 + core for step in range(1, RING)]
    along_z = [(lax.rem(deep + step, RING) * RING + row) * 2 + core for step in range(1, RING)]
    return core, row, deep, partner, along_y, along_z


def strip_sum(
    remote, strip, scale, meanwhile, src, src_half, pair_in, y_sum, y_out, y_in, z_out, z_in, gathered,
    pair_send, pair_recv, y_send, y_recv, z_send, z_recv, g_send, g_recv, p_send, p_recv,
):
    core, row, deep, partner, along_y, along_z = sum_peers(strip)
    mine = core * RING
    other = (1 - core) * RING
    order = sorted(range(1, RING), key=lambda step: -min(step, RING - step))
    pieces = [lax.rem(row + step, RING) for step in order] + [row]
    swaps = []
    for at, index in enumerate(pieces):
        src_half[other + index] = src[other + index].astype(jnp.bfloat16)
    for at, index in enumerate(pieces):
        copy = remote(
            src_half.at[other + index],
            pair_in.at[index],
            pair_send.at[at],
            pair_recv.at[at],
            partner,
        )
        copy.start()
        swaps.append(copy)
    scatter = [None] * (RING - 1)
    for at, index in enumerate(pieces):
        swaps[at].wait_recv()
        both = src[mine + index] + pair_in[index].astype(jnp.float32)
        if at == RING - 1:
            y_sum[...] = both
            break
        step = order[at]
        y_out[index] = both.astype(jnp.bfloat16)
        copy = remote(
            y_out.at[index],
            y_in.at[step - 1],
            y_send.at[step - 1],
            y_recv.at[step - 1],
            along_y[step - 1],
        )
        copy.start()
        scatter[step - 1] = copy
    meanwhile()
    total = y_sum[...]
    for step in range(1, RING):
        scatter[step - 1].wait_recv()
        total = total + y_in[step - 1].astype(jnp.float32)
    z_out[...] = total.astype(jnp.bfloat16)
    z_in[deep] = total.astype(jnp.bfloat16)
    trade = []
    for step in order:
        copy = remote(
            z_out, z_in.at[deep], z_send.at[step - 1], z_recv.at[step - 1], along_z[step - 1]
        )
        copy.start()
        trade.append(copy)
    for copy in trade:
        copy.wait_recv()
    total = z_in[0].astype(jnp.float32)
    for index in range(1, RING):
        total = total + z_in[index].astype(jnp.float32)
    own = mine + row
    gathered[own] = (total * scale).astype(jnp.bfloat16)
    gather = [None] * (RING - 1)
    for step in order:
        copy = remote(
            gathered.at[own],
            gathered.at[own],
            g_send.at[step - 1],
            g_recv.at[step - 1],
            along_y[step - 1],
        )
        copy.start()
        gather[step - 1] = copy
    passed = [
        remote(gathered.at[own], gathered.at[own], p_send.at[0], p_recv.at[0], partner)
    ]
    passed[0].start()
    for step in reversed(order):
        gather[step - 1].wait_recv()
        came = mine + lax.rem(row + RING - step, RING)
        copy = remote(
            gathered.at[came], gathered.at[came], p_send.at[step], p_recv.at[step], partner
        )
        copy.start()
        passed.append(copy)
    for copy in passed:
        copy.wait_recv()
    for copy in swaps + scatter + trade + gather + passed:
        copy.wait_send()


SECTIONS = 4
ROWS = 64
COLS = 32
CH = 64
GROUP = 4 * CH
SIDE = 2 * CH
BLOCK = 32
NARROW = 16
CHUNKS = (4, 3, 5, 4)
WAIT, INNER, OUTER = range(3)
STEPS = (
    ((INNER, 0, 4), (OUTER, 0, 3), (INNER, 4, 8), (OUTER, 3, 6), (OUTER, 6, 8)),
    ((WAIT, 0, 4), (INNER, 0, 3), (OUTER, 0, 2), (WAIT, 4, 6), (INNER, 3, 6), (OUTER, 2, 6)),
    ((WAIT, 0, 5), (INNER, 0, 5), (OUTER, 0, 5)),
    ((WAIT, 0, 4), (INNER, 0, 4)),
)


def plans():
    reach = [0] * SECTIONS
    for level in reversed(range(SECTIONS - 1)):
        reach[level] = (8 * (reach[level + 1] + 2) + 7) // 6
    result = []
    for level in range(SECTIONS):
        rows = ROWS * 3**level // 4**level
        cols = COLS * 3**level // 4**level
        halo = reach[level] + 4
        lead = halo
        tall = -(-(lead + rows + halo) // 16) * 16
        first = max(0, (rows - halo) // 16 * 16)
        first = min(first, ROWS - BLOCK)
        if rows - first > BLOCK:
            first += 16
        result.append(
            dict(
                rows=rows,
                cols=cols,
                reach=reach[level],
                halo=halo,
                lead=lead,
                tall=tall,
                groups=-(-cols // 4),
                first=first,
                sent=-(-(lead + rows + reach[level] + 2) // 8) * 8,
                chunk=CHUNKS[level],
                back=-(-(rows + 2 * halo - 2) // 16) * 16,
            )
        )
    return result


PLANS = plans()
TALL = max(plan["tall"] for plan in PLANS)
WIDE = max(plan["groups"] for plan in PLANS) * GROUP
NEXT_TALL = max(plan["tall"] for plan in PLANS[1:])
NEXT_WIDE = max(plan["groups"] for plan in PLANS[1:]) * GROUP
DEEP = max(plan["back"] * plan["groups"] for plan in PLANS)


def column_weights(level):
    fine, coarse = PLANS[level]["cols"], PLANS[level + 1]["cols"]
    table = {}
    for col in range(fine):
        num = max((2 * col + 1) * coarse - fine, 0)
        low = num // (2 * fine)
        frac = (num - 2 * fine * low) / (2 * fine)
        high = min(low + 1, coarse - 1)
        table[col, low] = table.get((col, low), 0.0) + 1.0 - frac
        table[col, high] = table.get((col, high), 0.0) + frac
    return {key: value for key, value in table.items() if value != 0.0}


def column_windows(level):
    table = column_weights(level)
    limit = PLANS[level]["groups"] * 4 - 8
    starts = []
    for group in range(PLANS[level + 1]["groups"]):
        used = [fine for fine, coarse in table if coarse // 4 == group]
        start = min(min(used) // 2 * 2, limit)
        assert max(used) < start + 8
        starts.append(start)
    return starts


def iota(shape, axis):
    return lax.broadcasted_iota(jnp.int32, shape, axis)


def mat(left, right):
    return jnp.dot(left, right, preferred_element_type=jnp.float32)


def steepness(value):
    half = 0.5 * (1.0 - LEAK)
    return (LEAK + half) + half * jnp.tanh(0.5 * value)


def one_hot(cond):
    return jnp.where(cond, 1.0, 0.0).astype(jnp.bfloat16)


def each_group(count, body, step):
    def run(index, carry):
        body([index * step + extra for extra in range(step)])
        return carry

    if step == count:
        body(list(range(count)))
    else:
        lax.fori_loop(0, count // step, run, 0)


def lanes(start, size):
    if isinstance(start, int):
        return pl.ds(start, size)
    return pl.ds(pl.multiple_of(start, 128), size)


def chain_body(
    x, cot, taps, bias, noise, sums_out,
    stack, stack_g, bands, x_b, h_b, eo_b, ei_b, slope_in, slope_out, g_b, back_b, up_b,
    row_b, g_out, g_in, cols_m, tall_x, tall_e, grid_a, bias_acc,
    packed, taps_v, bias_v, local_sem, x_send, x_recv, c_send, c_recv, g_send, g_recv, *sum_refs,
):
    section = lax.axis_index("section")
    strip = lax.axis_index("strip")
    strips = lax.axis_size("strip")
    below = lax.rem(strip + 1, strips)
    above = lax.rem(strip + strips - 1, strips)
    coarser = lax.rem(section + 1, SECTIONS)
    finer = lax.rem(section + SECTIONS - 1, SECTIONS)

    fetches = [
        pltpu.make_async_copy(taps, taps_v, local_sem.at[0]),
        pltpu.make_async_copy(bias, bias_v, local_sem.at[1]),
        pltpu.make_async_copy(x, stack.at[pl.ds(BLOCK, ROWS)], local_sem.at[2]),
        pltpu.make_async_copy(cot, stack_g.at[pl.ds(NARROW, ROWS)], local_sem.at[3]),
    ]
    for fetch in fetches:
        fetch.start()
    barrier = pltpu.get_barrier_semaphore()
    partner, along_y, along_z = sum_peers(strip)[3:]
    peers = [(section, below), (section, above), (coarser, strip), (finer, strip)]
    peers += [(section, peer) for peer in [partner] + along_y + along_z]
    for peer in peers:
        pl.semaphore_signal(barrier, inc=1, device_id=peer, device_id_type=MESH)

    bands[...] = jnp.zeros_like(bands)
    fetches[0].wait()
    blank = jnp.zeros((CH, CH), jnp.float32)
    for which, (source, flip) in enumerate(((0, False), (1, False), (1, True), (0, True))):
        for dy in range(3):
            tap_list = []
            for dx in range(3):
                at = (2 - dy) * 3 + 2 - dx if flip else dy * 3 + dx
                tap_list.append(taps_v[source, at].astype(jnp.float32))
            tap_list.append(blank)
            for index in range(4):
                pair = (tap_list[index], tap_list[index - 1])
                if flip:
                    block = jnp.concatenate(pair, axis=0).T
                else:
                    block = jnp.concatenate(pair, axis=1)
                block = block.astype(jnp.bfloat16)
                for half in range(2):
                    row = CH * (2 * half + 1 + index)
                    col = GROUP * dy + SIDE * half
                    bands[which, row : row + CH, col : col + SIDE] = block

    pl.semaphore_wait(barrier, len(peers))

    def remote(src_ref, dst_ref, send, recv, peer):
        return pltpu.make_async_remote_copy(
            src_ref=src_ref,
            dst_ref=dst_ref,
            send_sem=send,
            recv_sem=recv,
            device_id=peer,
            device_id_type=MESH,
        )

    first = PLANS[0]["first"]
    for level in range(1, SECTIONS):
        first = jnp.where(section >= level, PLANS[level]["first"], first)
    x_down = remote(
        x.at[pl.ds(pl.multiple_of(first, 16), BLOCK)],
        stack.at[pl.ds(0, BLOCK)],
        x_send.at[0],
        x_recv.at[0],
        (section, below),
    )
    x_up = remote(
        x.at[pl.ds(0, BLOCK)],
        stack.at[pl.ds(BLOCK + ROWS, BLOCK)],
        x_send.at[1],
        x_recv.at[1],
        (section, above),
    )
    c_down = remote(
        cot.at[pl.ds(ROWS - NARROW, NARROW)],
        stack_g.at[pl.ds(0, NARROW)],
        c_send.at[0],
        c_recv.at[0],
        (section, below),
    )
    c_up = remote(
        cot.at[pl.ds(0, NARROW)],
        stack_g.at[pl.ds(NARROW + ROWS, NARROW)],
        c_send.at[1],
        c_recv.at[1],
        (section, above),
    )
    x_down.start()
    x_up.start()

    @pl.when(section == 0)
    def _():
        c_down.start()
        c_up.start()

    for fetch in fetches[1:]:
        fetch.wait()
    bias_rows = jnp.concatenate([bias_v[...]] * 4, axis=1)

    def hop(level, group, peer):
        part = (pl.ds(0, PLANS[level]["sent"]), pl.ds(group * GROUP, GROUP))
        return remote(g_out.at[part], g_in.at[part], g_send.at[group], g_recv.at[group], peer)

    def live_of(level, group):
        lane = iota((PLANS[level]["tall"], GROUP), 1)
        return lane + group * GROUP < PLANS[level]["cols"] * CH

    def conv_of(tall, ref, which, group_list):
        windows = [ref[0:tall, lanes(group * GROUP, 2 * GROUP)] for group in group_list]
        three = mat(jnp.concatenate(windows, axis=0), bands[which])
        result = []
        for index in range(len(group_list)):
            part = three[index * tall : (index + 1) * tall]
            result.append(
                pltpu.roll(part[:, :GROUP], 1, 0)
                + part[:, GROUP : 2 * GROUP]
                + pltpu.roll(part[:, 2 * GROUP :], tall - 1, 0)
            )
        return zip(group_list, result)

    def save_noise(level):
        plan = PLANS[level]
        rows, back, groups = plan["rows"], plan["back"], plan["groups"]
        shape = (ROWS, back)
        choose = one_hot(
            (iota(shape, 1) == iota(shape, 0) + plan["lead"]) & (iota(shape, 0) < rows)
        )

        def save(group_list):
            for group in group_list:
                span_lanes = lanes(group * GROUP, GROUP)
                noise[:, span_lanes] = mat(choose, back_b[0:back, span_lanes]).astype(
                    jnp.bfloat16
                )

        each_group(groups, save, plan["chunk"])
        if groups * GROUP < COLS * CH:
            noise[:, groups * GROUP :] = jnp.zeros(
                (ROWS, COLS * CH - groups * GROUP), jnp.bfloat16
            )

    def finish_last():
        level = SECTIONS - 1
        back = PLANS[level]["back"]

        def back_last(group_list):
            for group, value in conv_of(back, ei_b, 3, group_list):
                value = jnp.where(live_of(level, group)[:back], value, 0.0)
                back_b[0:back, lanes(group * GROUP, GROUP)] = value.astype(jnp.bfloat16)

        each_group(PLANS[level]["groups"], back_last, PLANS[level]["chunk"])
        save_noise(level)

    def run_section(level):
        plan = PLANS[level]
        rows, lead, tall = plan["rows"], plan["lead"], plan["tall"]
        groups, chunk, back = plan["groups"], plan["chunk"], plan["back"]
        image = iota((tall, GROUP), 0) - lead
        keep_rows = ((image >= 0) | (strip > 0)) & ((image < rows) | (strip < strips - 1))
        inner_rows = (image[:back] >= 0) & (image[:back] < rows)

        def live(group):
            return live_of(level, group)

        def live_back(group):
            return iota((back, GROUP), 1) + group * GROUP < plan["cols"] * CH

        def conv(ref, which, group_list):
            return conv_of(tall, ref, which, group_list)

        def conv_back(ref, which, group_list):
            return conv_of(back, ref, which, group_list)

        def put(ref, group, value):
            size = value.shape[0]
            ref[0:size, lanes(SIDE + group * GROUP, GROUP)] = value.astype(jnp.bfloat16)

        for ref in (x_b, h_b, eo_b, ei_b):
            zero = jnp.zeros((tall, SIDE), jnp.bfloat16)
            ref[0:tall, 0:SIDE] = zero
            ref[0:tall, SIDE + groups * GROUP : 2 * SIDE + groups * GROUP] = zero

        if level + 1 < SECTIONS:
            table = column_weights(level)
            across = iota((CH, SIDE), 1) - iota((CH, SIDE), 0)
            for group, start in enumerate(column_windows(level)):
                for fine in range(8):
                    for half in range(2):
                        coarse = 4 * group + 2 * half
                        low = table.get((start + fine, coarse), 0.0)
                        high = table.get((start + fine, coarse + 1), 0.0)
                        block = jnp.where(across == 0, low, 0.0) + jnp.where(
                            across == CH, high, 0.0
                        )
                        cols_m[
                            group,
                            CH * fine : CH * fine + CH,
                            SIDE * half : SIDE * half + SIDE,
                        ] = block.astype(jnp.bfloat16)

        x_down.wait_recv()
        x_up.wait_recv()
        span = 2 * BLOCK + ROWS
        at = iota((tall, span), 0) - lead
        slot = iota((tall, span), 1)
        want = jnp.where(
            at < 0,
            at + rows - plan["first"],
            jnp.where(at < rows, at + BLOCK, at - rows + BLOCK + ROWS),
        )
        near = (at >= -plan["halo"]) & (at < rows + plan["halo"])
        near = near & ((at >= 0) | (strip > 0)) & ((at < rows) | (strip < strips - 1))
        pick = one_hot((slot == want) & near)

        def load_x(group_list):
            for group in group_list:
                value = mat(pick, stack[:, lanes(group * GROUP, GROUP)])
                put(x_b, group, jnp.where(live(group), value, 0.0))

        each_group(groups, load_x, chunk)

        def forward_in(group_list):
            for group, value in conv(x_b, 0, group_list):
                value = value + bias_rows[0:1, :]
                soft = jnp.maximum(value, 0.0) + jnp.log(1.0 + jnp.exp(-jnp.abs(value)))
                hidden = LEAK * value + (1.0 - LEAK) * soft
                keep = keep_rows & live(group)
                put(h_b, group, jnp.where(keep, hidden, 0.0))
                slope = jnp.where(keep, steepness(value), 0.0)
                slope_in[0:tall, lanes(group * GROUP, GROUP)] = slope

        each_group(groups, forward_in, chunk)

        def forward_out(group_list):
            for group, value in conv(h_b, 1, group_list):
                value = value + bias_rows[1:2, :]
                slope = jnp.where(live(group), steepness(value), 0.0)
                slope_out[0:tall, lanes(group * GROUP, GROUP)] = slope

        each_group(groups, forward_out, chunk)

        if level == 0:
            c_down.wait_recv()
            c_up.wait_recv()
            span_g = 2 * NARROW + ROWS
            at_g = iota((back, span_g), 0) - lead
            near_g = ((at_g >= 0) | (strip > 0)) & ((at_g < rows) | (strip < strips - 1))
            pick_g = one_hot((iota((back, span_g), 1) == at_g + NARROW) & near_g)

            def load_g(group_list):
                for group in group_list:
                    span_lanes = lanes(group * GROUP, GROUP)
                    value = mat(pick_g, stack_g[:, span_lanes])
                    g_b[0:back, span_lanes] = value
                    put(eo_b, group, value * slope_out[0:back, span_lanes])

            each_group(groups, load_g, chunk)
        else:
            sent = min(plan["sent"], back)

            def arrive(group_list):
                for group in group_list:
                    hop(level, group, (finer, strip)).wait_recv()
                    span_lanes = lanes(group * GROUP, GROUP)
                    value = g_in[0:sent, span_lanes].astype(jnp.float32)
                    if sent < back:
                        rest = jnp.zeros((back - sent, GROUP), jnp.float32)
                        value = jnp.concatenate([value, rest], axis=0)
                    g_b[0:back, span_lanes] = value
                    put(eo_b, group, value * slope_out[0:back, span_lanes])

        def error_in(group_list):
            for group, value in conv_back(eo_b, 2, group_list):
                put(ei_b, group, value * slope_in[0:back, lanes(group * GROUP, GROUP)])

        def back_input(group_list):
            for group, value in conv_back(ei_b, 3, group_list):
                span_lanes = lanes(group * GROUP, GROUP)
                value = jnp.where(live_back(group), value, 0.0)
                back_b[0:back, span_lanes] = value.astype(jnp.bfloat16)
                total = g_b[0:back, span_lanes] + value
                up_b[0:back, span_lanes] = total.astype(jnp.bfloat16)

        if level + 1 < SECTIONS:
            after = PLANS[level + 1]
            shape = (after["tall"], back)
            coarse_row = strip * after["rows"] + iota(shape, 0) - after["lead"]
            local_row = iota(shape, 1) - lead
            fine_row = strip * rows + local_row
            num = jnp.maximum(6 * fine_row - 1, 0)
            low = num >> 3
            frac = (num & 7).astype(jnp.float32) * 0.125
            high = jnp.minimum(low + 1, strips * after["rows"] - 1)
            real = (fine_row >= 0) & (fine_row < strips * rows)
            real = real & (local_row >= -plan["reach"]) & (local_row < rows + plan["reach"])
            real = real & (coarse_row >= 0) & (coarse_row < strips * after["rows"])
            row_m = jnp.where(coarse_row == low, 1.0 - frac, 0.0)
            row_m = row_m + jnp.where(coarse_row == high, frac, 0.0)
            row_m = jnp.where(real, row_m, 0.0).astype(jnp.bfloat16)

            windows = column_windows(level)

        ready = 0
        for kind, begin, end in STEPS[level]:
            part = list(range(begin, end))
            if kind == WAIT:
                arrive(part)
            elif kind == INNER:
                error_in(part)
            else:
                back_input(part)
                for group in part:
                    span_lanes = lanes(group * GROUP, GROUP)
                    value = mat(row_m, up_b[0:back, span_lanes])
                    row_b[0 : after["tall"], span_lanes] = value.astype(jnp.bfloat16)
                while ready < len(windows) and windows[ready] + 8 <= 4 * end:
                    start = CH * windows[ready]
                    value = mat(
                        row_b[0 : after["tall"], start : start + 2 * GROUP], cols_m[ready]
                    )
                    g_out[0 : after["tall"], GROUP * ready : GROUP * ready + GROUP] = (
                        value.astype(jnp.bfloat16)
                    )
                    hop(level + 1, ready, (coarser, strip)).start()
                    ready += 1

        if level + 1 < SECTIONS:
            save_noise(level)

        for which, (field, error) in enumerate(((x_b, ei_b), (h_b, eo_b))):
            bias_acc[which : which + 1, :] = jnp.zeros((1, GROUP), jnp.float32)

            def pile(group_list):
                for group in group_list:
                    if isinstance(group, int):
                        where_rows = pl.ds(group * back, back)
                    else:
                        where_rows = pl.ds(pl.multiple_of(group * back, 16), back)
                    tall_x[where_rows, :] = field[0:back, lanes(group * GROUP, 2 * GROUP)]
                    value = error[0:back, lanes(SIDE + group * GROUP, GROUP)]
                    value = jnp.where(inner_rows, value.astype(jnp.float32), 0.0)
                    bias_acc[which : which + 1, :] += jnp.sum(value, axis=0, keepdims=True)
                    tall_e[where_rows, 0:GROUP] = pltpu.roll(value, back - 1, 0).astype(
                        jnp.bfloat16
                    )
                    tall_e[where_rows, GROUP : 2 * GROUP] = value.astype(jnp.bfloat16)
                    tall_e[where_rows, 2 * GROUP :] = pltpu.roll(value, 1, 0).astype(
                        jnp.bfloat16
                    )

            each_group(groups, pile, chunk)
            grid_a[which] = lax.dot_general(
                tall_x[0 : groups * back, :],
                tall_e[0 : groups * back, :],
                (((0,), (0,)), ((), ())),
                preferred_element_type=jnp.float32,
            )

    for level in range(SECTIONS):

        @pl.when(section == level)
        def _():
            run_section(level)

    def folded(which, tap):
        dy, dx = tap // 3, tap % 3
        low, high = 0.0, 0.0
        for half in range(2):
            span_lanes = slice(GROUP * dy + SIDE * half, GROUP * dy + SIDE * half + SIDE)
            row = CH * (2 * half + dx + 1)
            low = low + grid_a[which, row : row + CH, span_lanes]
            high = high + grid_a[which, row + CH : row + 2 * CH, span_lanes]
        return low, high

    left = iota((CH, SIDE), 1) < CH
    blocks = []
    for pair in range(9):
        low_a, high_a = folded((2 * pair) // 9, (2 * pair) % 9)
        low_b, high_b = folded((2 * pair + 1) // 9, (2 * pair + 1) % 9)
        blocks.append(
            jnp.where(left, low_a + pltpu.roll(high_a, CH, 1), high_b + pltpu.roll(low_b, CH, 1))
        )
    sums = bias_acc[:, 0:SIDE] + bias_acc[:, SIDE:]
    sums = sums + pltpu.roll(sums, CH, 1)
    tail = jnp.where(iota((8, SIDE), 1) < CH, sums[0:1, :], sums[1:2, :])
    blocks.append(jnp.where(iota((8, SIDE), 0) == 0, tail, 0.0))
    blocks.append(jnp.zeros((PIECES * PIECE - 9 * CH - 8, SIDE), jnp.float32))
    packed[...] = jnp.concatenate(blocks, axis=0).reshape(PIECES, PIECE, SIDE)

    scale = 0.0
    for level, plan in enumerate(PLANS):
        factor = 1.0 / math.sqrt(strips * plan["rows"] * plan["cols"])
        scale = jnp.where(section == level, jnp.float32(factor), scale)

    def meanwhile():
        @pl.when(section == SECTIONS - 1)
        def _():
            finish_last()

    strip_sum(
        lambda a, b, c, d, peer: remote(a, b, c, d, (section, peer)),
        strip,
        scale,
        meanwhile,
        packed,
        *sum_refs,
    )
    sums_out[...] = sum_refs[7][...]

    x_down.wait_send()
    x_up.wait_send()

    @pl.when(section == 0)
    def _():
        c_down.wait_send()
        c_up.wait_send()

    for level in range(1, SECTIONS):

        @pl.when(section == level - 1)
        def _():
            for group in range(PLANS[level]["groups"]):
                hop(level, group, (coarser, strip)).wait_send()


def chain(x, cot, taps, bias):
    dma = pltpu.SemaphoreType.DMA
    half, full = jnp.bfloat16, jnp.float32
    padded = WIDE + 2 * SIDE
    in_vmem = pl.BlockSpec(memory_space=pltpu.VMEM)
    return pl.pallas_call(
        chain_body,
        out_shape=(
            jax.ShapeDtypeStruct((ROWS, COLS * CH), half),
            jax.ShapeDtypeStruct((PIECES, PIECE, SIDE), half),
        ),
        in_specs=[pl.BlockSpec(memory_space=pltpu.HBM)] * 4,
        out_specs=(in_vmem, in_vmem),
        scratch_shapes=[
            pltpu.VMEM((2 * BLOCK + ROWS, COLS * CH), half),
            pltpu.VMEM((2 * NARROW + ROWS, COLS * CH), half),
            pltpu.VMEM((4, 2 * GROUP, 3 * GROUP), half),
            pltpu.VMEM((TALL, padded), half),
            pltpu.VMEM((TALL, padded), half),
            pltpu.VMEM((TALL, padded), half),
            pltpu.VMEM((TALL, padded), half),
            pltpu.VMEM((TALL, WIDE), full),
            pltpu.VMEM((TALL, WIDE), full),
            pltpu.VMEM((TALL, WIDE), full),
            pltpu.VMEM((TALL, WIDE), half),
            pltpu.VMEM((TALL, WIDE), half),
            pltpu.VMEM((NEXT_TALL, WIDE), half),
            pltpu.VMEM((NEXT_TALL, NEXT_WIDE), half),
            pltpu.VMEM((NEXT_TALL, NEXT_WIDE), half),
            pltpu.VMEM((NEXT_WIDE // GROUP, 2 * GROUP, GROUP), half),
            pltpu.VMEM((DEEP, 2 * GROUP), half),
            pltpu.VMEM((DEEP, 3 * GROUP), half),
            pltpu.VMEM((2, 2 * GROUP, 3 * GROUP), full),
            pltpu.VMEM((2, GROUP), full),
            pltpu.VMEM((PIECES, PIECE, SIDE), full),
            pltpu.VMEM((2, 9, CH, CH), half),
            pltpu.VMEM((2, CH), full),
            dma((4,)),
            dma((2,)), dma((2,)), dma((2,)), dma((2,)),
            dma((NEXT_WIDE // GROUP,)), dma((NEXT_WIDE // GROUP,)),
            pltpu.VMEM((PIECES, PIECE, SIDE), half),
            pltpu.VMEM((RING, PIECE, SIDE), half),
            pltpu.VMEM((PIECE, SIDE), full),
            pltpu.VMEM((RING, PIECE, SIDE), half),
            pltpu.VMEM((RING - 1, PIECE, SIDE), half),
            pltpu.VMEM((PIECE, SIDE), half),
            pltpu.VMEM((RING, PIECE, SIDE), half),
            pltpu.VMEM((PIECES, PIECE, SIDE), half),
            dma((RING,)), dma((RING,)),
            dma((RING - 1,)), dma((RING - 1,)),
            dma((RING - 1,)), dma((RING - 1,)),
            dma((RING - 1,)), dma((RING - 1,)),
            dma((RING,)), dma((RING,)),
        ],
        compiler_params=pltpu.CompilerParams(
            collective_id=0, has_side_effects=True, vmem_limit_bytes=67043328
        ),
    )(x, cot, taps, bias)


def write_body(noise_in, sums_in, noise, kernel_out, bias_out, final):
    noise[...] = noise_in[...]
    final[...] = sums_in[...].astype(jnp.float32).reshape(PIECES * PIECE, SIDE)
    for pair in range(9):
        block = final[CH * pair : CH * pair + CH, :]
        kernel_out[2 * pair] = block[:, :CH]
        kernel_out[2 * pair + 1] = pltpu.roll(block, CH, 1)[:, :CH]
    sums = final[9 * CH : 9 * CH + 8, :]
    bias_out[0:1, :] = sums[0:1, :CH]
    bias_out[1:2, :] = pltpu.roll(sums, CH, 1)[0:1, :CH]


def write_out(noise, sums):
    in_vmem = pl.BlockSpec(memory_space=pltpu.VMEM)
    full = jnp.float32
    return pl.pallas_call(
        write_body,
        out_shape=(
            jax.ShapeDtypeStruct(noise.shape, noise.dtype),
            jax.ShapeDtypeStruct((18, CH, CH), full),
            jax.ShapeDtypeStruct((2, CH), full),
        ),
        in_specs=[in_vmem] * 2,
        out_specs=(in_vmem,) * 3,
        scratch_shapes=[pltpu.VMEM((PIECES * PIECE, SIDE), full)],
        compiler_params=pltpu.CompilerParams(vmem_limit_bytes=67043328),
    )(noise, sums)


def local(cotangent, activations, weights, biases):
    taps = weights.reshape(2, 9, CH, CH)
    noise, sums = chain(activations[0, 0], cotangent[0], taps, biases[0])
    noise, kernels, sums = write_out(noise, sums)
    return (
        noise[None, None],
        kernels.reshape(1, 2, 3, 3, CH, CH),
        sums[None],
    )


def solution(mesh):
    return jax.shard_map(
        local,
        mesh=mesh,
        in_specs=(
            P(None, "strip", None),
            P("section", None, "strip", None),
            P("section", None, None, None, None, None),
            P("section", None, None),
        ),
        out_specs=(
            P("section", None, "strip", None),
            P("section", None, None, None, None, None),
            P("section", None, None),
        ),
        check_vma=False,
    )
```

```python
import math

import jax
import jax.numpy as jnp
from jax import lax
from jax.experimental import pallas as pl
from jax.experimental.pallas import tpu as pltpu
from jax.sharding import PartitionSpec as P

LEAK = 0.05
RING = 8
PIECE = 40
PIECES = 2 * RING
MESH = pl.DeviceIdType.MESH


def sum_peers(strip):
    core = lax.rem(strip, 2)
    row = lax.rem(lax.div(strip, 2), RING)
    deep = lax.div(strip, 2 * RING)
    partner = strip + 1 - 2 * core
    along_y = [(deep * RING + lax.rem(row + step, RING)) * 2 + core for step in range(1, RING)]
    along_z = [(lax.rem(deep + step, RING) * RING + row) * 2 + core for step in range(1, RING)]
    return core, row, deep, partner, along_y, along_z


def strip_sum(
    remote, strip, scale, meanwhile, src, src_half, pair_in, y_sum, y_out, y_in, z_out, z_in, gathered,
    pair_send, pair_recv, y_send, y_recv, z_send, z_recv, g_send, g_recv, p_send, p_recv,
):
    core, row, deep, partner, along_y, along_z = sum_peers(strip)
    mine = core * RING
    other = (1 - core) * RING
    order = sorted(range(1, RING), key=lambda step: -min(step, RING - step))
    pieces = [lax.rem(row + step, RING) for step in order] + [row]
    swaps = []
    for at, index in enumerate(pieces):
        src_half[other + index] = src[other + index].astype(jnp.bfloat16)
    for at, index in enumerate(pieces):
        copy = remote(
            src_half.at[other + index],
            pair_in.at[index],
            pair_send.at[at],
            pair_recv.at[at],
            partner,
        )
        copy.start()
        swaps.append(copy)
    scatter = [None] * (RING - 1)
    for at, index in enumerate(pieces):
        swaps[at].wait_recv()
        both = src[mine + index] + pair_in[index].astype(jnp.float32)
        if at == RING - 1:
            y_sum[...] = both
            break
        step = order[at]
        y_out[index] = both.astype(jnp.bfloat16)
        copy = remote(
            y_out.at[index],
            y_in.at[step - 1],
            y_send.at[step - 1],
            y_recv.at[step - 1],
            along_y[step - 1],
        )
        copy.start()
        scatter[step - 1] = copy
    meanwhile()
    total = y_sum[...]
    for step in range(1, RING):
        scatter[step - 1].wait_recv()
        total = total + y_in[step - 1].astype(jnp.float32)
    z_out[...] = total.astype(jnp.bfloat16)
    z_in[deep] = total.astype(jnp.bfloat16)
    trade = []
    for step in order:
        copy = remote(
            z_out, z_in.at[deep], z_send.at[step - 1], z_recv.at[step - 1], along_z[step - 1]
        )
        copy.start()
        trade.append(copy)
    for copy in trade:
        copy.wait_recv()
    total = z_in[0].astype(jnp.float32)
    for index in range(1, RING):
        total = total + z_in[index].astype(jnp.float32)
    own = mine + row
    gathered[own] = (total * scale).astype(jnp.bfloat16)
    gather = [None] * (RING - 1)
    for step in order:
        copy = remote(
            gathered.at[own],
            gathered.at[own],
            g_send.at[step - 1],
            g_recv.at[step - 1],
            along_y[step - 1],
        )
        copy.start()
        gather[step - 1] = copy
    passed = [
        remote(gathered.at[own], gathered.at[own], p_send.at[0], p_recv.at[0], partner)
    ]
    passed[0].start()
    for step in reversed(order):
        gather[step - 1].wait_recv()
        came = mine + lax.rem(row + RING - step, RING)
        copy = remote(
            gathered.at[came], gathered.at[came], p_send.at[step], p_recv.at[step], partner
        )
        copy.start()
        passed.append(copy)
    for copy in passed:
        copy.wait_recv()
    for copy in swaps + scatter + trade + gather + passed:
        copy.wait_send()


SECTIONS = 4
ROWS = 64
COLS = 32
CH = 64
GROUP = 4 * CH
SIDE = 2 * CH
BLOCK = 32
NARROW = 16
CHUNKS = (4, 3, 5, 4)
WAIT, INNER, OUTER = range(3)
STEPS = (
    ((INNER, 0, 4), (OUTER, 0, 3), (INNER, 4, 8), (OUTER, 3, 6), (OUTER, 6, 8)),
    (
        (WAIT, 0, 4), (INNER, 0, 3), (OUTER, 0, 2),
        (WAIT, 4, 6), (INNER, 3, 6), (OUTER, 2, 4), (OUTER, 4, 6),
    ),
    ((WAIT, 0, 3), (INNER, 0, 2), (WAIT, 3, 5), (INNER, 2, 5), (OUTER, 0, 3), (OUTER, 3, 5)),
    ((WAIT, 0, 4), (INNER, 0, 4)),
)


def plans():
    reach = [0] * SECTIONS
    for level in reversed(range(SECTIONS - 1)):
        reach[level] = (8 * (reach[level + 1] + 2) + 7) // 6
    result = []
    for level in range(SECTIONS):
        rows = ROWS * 3**level // 4**level
        cols = COLS * 3**level // 4**level
        halo = reach[level] + 4
        lead = halo
        tall = -(-(lead + rows + halo) // 16) * 16
        first = max(0, (rows - halo) // 16 * 16)
        first = min(first, ROWS - BLOCK)
        if rows - first > BLOCK:
            first += 16
        result.append(
            dict(
                rows=rows,
                cols=cols,
                reach=reach[level],
                halo=halo,
                lead=lead,
                tall=tall,
                groups=-(-cols // 4),
                first=first,
                sent=-(-(lead + rows + reach[level] + 2) // 8) * 8,
                chunk=CHUNKS[level],
                back=-(-(rows + 2 * halo - 2) // 16) * 16,
            )
        )
    return result


PLANS = plans()
TALL = max(plan["tall"] for plan in PLANS)
WIDE = max(plan["groups"] for plan in PLANS) * GROUP
NEXT_TALL = max(plan["tall"] for plan in PLANS[1:])
NEXT_WIDE = max(plan["groups"] for plan in PLANS[1:]) * GROUP
DEEP = max(plan["back"] * plan["groups"] for plan in PLANS)


def column_weights(level):
    fine, coarse = PLANS[level]["cols"], PLANS[level + 1]["cols"]
    table = {}
    for col in range(fine):
        num = max((2 * col + 1) * coarse - fine, 0)
        low = num // (2 * fine)
        frac = (num - 2 * fine * low) / (2 * fine)
        high = min(low + 1, coarse - 1)
        table[col, low] = table.get((col, low), 0.0) + 1.0 - frac
        table[col, high] = table.get((col, high), 0.0) + frac
    return {key: value for key, value in table.items() if value != 0.0}


def column_windows(level):
    table = column_weights(level)
    limit = PLANS[level]["groups"] * 4 - 8
    starts = []
    for group in range(PLANS[level + 1]["groups"]):
        used = [fine for fine, coarse in table if coarse // 4 == group]
        start = min(min(used) // 2 * 2, limit)
        assert max(used) < start + 8
        starts.append(start)
    return starts


def iota(shape, axis):
    return lax.broadcasted_iota(jnp.int32, shape, axis)


def mat(left, right):
    return jnp.dot(left, right, preferred_element_type=jnp.float32)


def steepness(value):
    half = 0.5 * (1.0 - LEAK)
    return (LEAK + half) + half * jnp.tanh(0.5 * value)


def one_hot(cond):
    return jnp.where(cond, 1.0, 0.0).astype(jnp.bfloat16)


def each_group(count, body, step):
    def run(index, carry):
        body([index * step + extra for extra in range(step)])
        return carry

    if step == count:
        body(list(range(count)))
    else:
        lax.fori_loop(0, count // step, run, 0)


def lanes(start, size):
    if isinstance(start, int):
        return pl.ds(start, size)
    return pl.ds(pl.multiple_of(start, 128), size)


def chain_body(
    x, cot, taps, bias, noise, sums_out,
    stack, stack_g, bands, x_b, h_b, eo_b, ei_b, slope_in, slope_out, g_b, back_b, up_b,
    row_b, g_out, g_in, cols_m, tall_x, tall_e, grid_a, bias_acc,
    packed, taps_v, bias_v, local_sem, x_send, x_recv, c_send, c_recv, g_send, g_recv, *sum_refs,
):
    section = lax.axis_index("section")
    strip = lax.axis_index("strip")
    strips = lax.axis_size("strip")
    below = lax.rem(strip + 1, strips)
    above = lax.rem(strip + strips - 1, strips)
    coarser = lax.rem(section + 1, SECTIONS)
    finer = lax.rem(section + SECTIONS - 1, SECTIONS)

    fetches = [
        pltpu.make_async_copy(taps, taps_v, local_sem.at[0]),
        pltpu.make_async_copy(bias, bias_v, local_sem.at[1]),
        pltpu.make_async_copy(x, stack.at[pl.ds(BLOCK, ROWS)], local_sem.at[2]),
        pltpu.make_async_copy(cot, stack_g.at[pl.ds(NARROW, ROWS)], local_sem.at[3]),
    ]
    for fetch in fetches:
        fetch.start()
    barrier = pltpu.get_barrier_semaphore()
    partner, along_y, along_z = sum_peers(strip)[3:]
    peers = [(section, below), (section, above), (coarser, strip), (finer, strip)]
    peers += [(section, peer) for peer in [partner] + along_y + along_z]
    for peer in peers:
        pl.semaphore_signal(barrier, inc=1, device_id=peer, device_id_type=MESH)

    bands[...] = jnp.zeros_like(bands)
    fetches[0].wait()
    blank = jnp.zeros((CH, CH), jnp.float32)
    for which, (source, flip) in enumerate(((0, False), (1, False), (1, True), (0, True))):
        for dy in range(3):
            tap_list = []
            for dx in range(3):
                at = (2 - dy) * 3 + 2 - dx if flip else dy * 3 + dx
                tap_list.append(taps_v[source, at].astype(jnp.float32))
            tap_list.append(blank)
            for index in range(4):
                pair = (tap_list[index], tap_list[index - 1])
                if flip:
                    block = jnp.concatenate(pair, axis=0).T
                else:
                    block = jnp.concatenate(pair, axis=1)
                block = block.astype(jnp.bfloat16)
                for half in range(2):
                    row = CH * (2 * half + 1 + index)
                    col = GROUP * dy + SIDE * half
                    bands[which, row : row + CH, col : col + SIDE] = block

    pl.semaphore_wait(barrier, len(peers))

    def remote(src_ref, dst_ref, send, recv, peer):
        return pltpu.make_async_remote_copy(
            src_ref=src_ref,
            dst_ref=dst_ref,
            send_sem=send,
            recv_sem=recv,
            device_id=peer,
            device_id_type=MESH,
        )

    first = PLANS[0]["first"]
    for level in range(1, SECTIONS):
        first = jnp.where(section >= level, PLANS[level]["first"], first)
    x_down = remote(
        x.at[pl.ds(pl.multiple_of(first, 16), BLOCK)],
        stack.at[pl.ds(0, BLOCK)],
        x_send.at[0],
        x_recv.at[0],
        (section, below),
    )
    x_up = remote(
        x.at[pl.ds(0, BLOCK)],
        stack.at[pl.ds(BLOCK + ROWS, BLOCK)],
        x_send.at[1],
        x_recv.at[1],
        (section, above),
    )
    c_down = remote(
        cot.at[pl.ds(ROWS - NARROW, NARROW)],
        stack_g.at[pl.ds(0, NARROW)],
        c_send.at[0],
        c_recv.at[0],
        (section, below),
    )
    c_up = remote(
        cot.at[pl.ds(0, NARROW)],
        stack_g.at[pl.ds(NARROW + ROWS, NARROW)],
        c_send.at[1],
        c_recv.at[1],
        (section, above),
    )
    x_down.start()
    x_up.start()

    @pl.when(section == 0)
    def _():
        c_down.start()
        c_up.start()

    for fetch in fetches[1:]:
        fetch.wait()
    bias_rows = jnp.concatenate([bias_v[...]] * 4, axis=1)

    def hop(level, group, peer):
        part = (pl.ds(0, PLANS[level]["sent"]), pl.ds(group * GROUP, GROUP))
        return remote(g_out.at[part], g_in.at[part], g_send.at[group], g_recv.at[group], peer)

    def live_of(level, group):
        lane = iota((PLANS[level]["tall"], GROUP), 1)
        return lane + group * GROUP < PLANS[level]["cols"] * CH

    def conv_of(tall, ref, which, group_list):
        windows = [ref[0:tall, lanes(group * GROUP, 2 * GROUP)] for group in group_list]
        three = mat(jnp.concatenate(windows, axis=0), bands[which])
        result = []
        for index in range(len(group_list)):
            part = three[index * tall : (index + 1) * tall]
            result.append(
                pltpu.roll(part[:, :GROUP], 1, 0)
                + part[:, GROUP : 2 * GROUP]
                + pltpu.roll(part[:, 2 * GROUP :], tall - 1, 0)
            )
        return zip(group_list, result)

    def save_noise(level):
        plan = PLANS[level]
        rows, back, groups = plan["rows"], plan["back"], plan["groups"]
        shape = (ROWS, back)
        choose = one_hot(
            (iota(shape, 1) == iota(shape, 0) + plan["lead"]) & (iota(shape, 0) < rows)
        )

        def save(group_list):
            for group in group_list:
                span_lanes = lanes(group * GROUP, GROUP)
                noise[:, span_lanes] = mat(choose, back_b[0:back, span_lanes]).astype(
                    jnp.bfloat16
                )

        each_group(groups, save, plan["chunk"])
        if groups * GROUP < COLS * CH:
            noise[:, groups * GROUP :] = jnp.zeros(
                (ROWS, COLS * CH - groups * GROUP), jnp.bfloat16
            )

    def finish_last():
        level = SECTIONS - 1
        back = PLANS[level]["back"]

        def back_last(group_list):
            for group, value in conv_of(back, ei_b, 3, group_list):
                value = jnp.where(live_of(level, group)[:back], value, 0.0)
                back_b[0:back, lanes(group * GROUP, GROUP)] = value.astype(jnp.bfloat16)

        each_group(PLANS[level]["groups"], back_last, PLANS[level]["chunk"])
        save_noise(level)

    def run_section(level):
        plan = PLANS[level]
        rows, lead, tall = plan["rows"], plan["lead"], plan["tall"]
        groups, chunk, back = plan["groups"], plan["chunk"], plan["back"]
        image = iota((tall, GROUP), 0) - lead
        keep_rows = ((image >= 0) | (strip > 0)) & ((image < rows) | (strip < strips - 1))
        inner_rows = (image[:back] >= 0) & (image[:back] < rows)

        def live(group):
            return live_of(level, group)

        def live_back(group):
            return iota((back, GROUP), 1) + group * GROUP < plan["cols"] * CH

        def conv(ref, which, group_list):
            return conv_of(tall, ref, which, group_list)

        def conv_back(ref, which, group_list):
            return conv_of(back, ref, which, group_list)

        def put(ref, group, value):
            size = value.shape[0]
            ref[0:size, lanes(SIDE + group * GROUP, GROUP)] = value.astype(jnp.bfloat16)

        for ref in (x_b, h_b, eo_b, ei_b):
            zero = jnp.zeros((tall, SIDE), jnp.bfloat16)
            ref[0:tall, 0:SIDE] = zero
            ref[0:tall, SIDE + groups * GROUP : 2 * SIDE + groups * GROUP] = zero

        if level + 1 < SECTIONS:
            table = column_weights(level)
            across = iota((CH, SIDE), 1) - iota((CH, SIDE), 0)
            for group, start in enumerate(column_windows(level)):
                for fine in range(8):
                    for half in range(2):
                        coarse = 4 * group + 2 * half
                        low = table.get((start + fine, coarse), 0.0)
                        high = table.get((start + fine, coarse + 1), 0.0)
                        block = jnp.where(across == 0, low, 0.0) + jnp.where(
                            across == CH, high, 0.0
                        )
                        cols_m[
                            group,
                            CH * fine : CH * fine + CH,
                            SIDE * half : SIDE * half + SIDE,
                        ] = block.astype(jnp.bfloat16)

        x_down.wait_recv()
        x_up.wait_recv()
        span = 2 * BLOCK + ROWS
        at = iota((tall, span), 0) - lead
        slot = iota((tall, span), 1)
        want = jnp.where(
            at < 0,
            at + rows - plan["first"],
            jnp.where(at < rows, at + BLOCK, at - rows + BLOCK + ROWS),
        )
        near = (at >= -plan["halo"]) & (at < rows + plan["halo"])
        near = near & ((at >= 0) | (strip > 0)) & ((at < rows) | (strip < strips - 1))
        pick = one_hot((slot == want) & near)

        def load_x(group_list):
            for group in group_list:
                value = mat(pick, stack[:, lanes(group * GROUP, GROUP)])
                put(x_b, group, jnp.where(live(group), value, 0.0))

        each_group(groups, load_x, chunk)

        def forward_in(group_list):
            for group, value in conv(x_b, 0, group_list):
                value = value + bias_rows[0:1, :]
                soft = jnp.maximum(value, 0.0) + jnp.log(1.0 + jnp.exp(-jnp.abs(value)))
                hidden = LEAK * value + (1.0 - LEAK) * soft
                keep = keep_rows & live(group)
                put(h_b, group, jnp.where(keep, hidden, 0.0))
                slope = jnp.where(keep, steepness(value), 0.0)
                slope_in[0:tall, lanes(group * GROUP, GROUP)] = slope

        each_group(groups, forward_in, chunk)

        def forward_out(group_list):
            for group, value in conv(h_b, 1, group_list):
                value = value + bias_rows[1:2, :]
                slope = jnp.where(live(group), steepness(value), 0.0)
                slope_out[0:tall, lanes(group * GROUP, GROUP)] = slope

        each_group(groups, forward_out, chunk)

        if level == 0:
            c_down.wait_recv()
            c_up.wait_recv()
            span_g = 2 * NARROW + ROWS
            at_g = iota((back, span_g), 0) - lead
            near_g = ((at_g >= 0) | (strip > 0)) & ((at_g < rows) | (strip < strips - 1))
            pick_g = one_hot((iota((back, span_g), 1) == at_g + NARROW) & near_g)

            def load_g(group_list):
                for group in group_list:
                    span_lanes = lanes(group * GROUP, GROUP)
                    value = mat(pick_g, stack_g[:, span_lanes])
                    g_b[0:back, span_lanes] = value
                    put(eo_b, group, value * slope_out[0:back, span_lanes])

            each_group(groups, load_g, chunk)
        else:
            sent = min(plan["sent"], back)

            def arrive(group_list):
                for group in group_list:
                    hop(level, group, (finer, strip)).wait_recv()
                    span_lanes = lanes(group * GROUP, GROUP)
                    value = g_in[0:sent, span_lanes].astype(jnp.float32)
                    if sent < back:
                        rest = jnp.zeros((back - sent, GROUP), jnp.float32)
                        value = jnp.concatenate([value, rest], axis=0)
                    g_b[0:back, span_lanes] = value
                    put(eo_b, group, value * slope_out[0:back, span_lanes])

        def error_in(group_list):
            for group, value in conv_back(eo_b, 2, group_list):
                put(ei_b, group, value * slope_in[0:back, lanes(group * GROUP, GROUP)])

        def back_input(group_list):
            for group, value in conv_back(ei_b, 3, group_list):
                span_lanes = lanes(group * GROUP, GROUP)
                value = jnp.where(live_back(group), value, 0.0)
                back_b[0:back, span_lanes] = value.astype(jnp.bfloat16)
                total = g_b[0:back, span_lanes] + value
                up_b[0:back, span_lanes] = total.astype(jnp.bfloat16)

        if level + 1 < SECTIONS:
            after = PLANS[level + 1]
            shape = (after["tall"], back)
            coarse_row = strip * after["rows"] + iota(shape, 0) - after["lead"]
            local_row = iota(shape, 1) - lead
            fine_row = strip * rows + local_row
            num = jnp.maximum(6 * fine_row - 1, 0)
            low = num >> 3
            frac = (num & 7).astype(jnp.float32) * 0.125
            high = jnp.minimum(low + 1, strips * after["rows"] - 1)
            real = (fine_row >= 0) & (fine_row < strips * rows)
            real = real & (local_row >= -plan["reach"]) & (local_row < rows + plan["reach"])
            real = real & (coarse_row >= 0) & (coarse_row < strips * after["rows"])
            row_m = jnp.where(coarse_row == low, 1.0 - frac, 0.0)
            row_m = row_m + jnp.where(coarse_row == high, frac, 0.0)
            row_m = jnp.where(real, row_m, 0.0).astype(jnp.bfloat16)

            windows = column_windows(level)

        ready = 0
        for kind, begin, end in STEPS[level]:
            part = list(range(begin, end))
            if kind == WAIT:
                arrive(part)
            elif kind == INNER:
                error_in(part)
            else:
                back_input(part)
                for group in part:
                    span_lanes = lanes(group * GROUP, GROUP)
                    value = mat(row_m, up_b[0:back, span_lanes])
                    row_b[0 : after["tall"], span_lanes] = value.astype(jnp.bfloat16)
                while ready < len(windows) and windows[ready] + 8 <= 4 * end:
                    start = CH * windows[ready]
                    value = mat(
                        row_b[0 : after["tall"], start : start + 2 * GROUP], cols_m[ready]
                    )
                    g_out[0 : after["tall"], GROUP * ready : GROUP * ready + GROUP] = (
                        value.astype(jnp.bfloat16)
                    )
                    hop(level + 1, ready, (coarser, strip)).start()
                    ready += 1

        if level + 1 < SECTIONS:
            save_noise(level)

        for which, (field, error) in enumerate(((x_b, ei_b), (h_b, eo_b))):
            bias_acc[which : which + 1, :] = jnp.zeros((1, GROUP), jnp.float32)

            def pile(group_list):
                for group in group_list:
                    if isinstance(group, int):
                        where_rows = pl.ds(group * back, back)
                    else:
                        where_rows = pl.ds(pl.multiple_of(group * back, 16), back)
                    tall_x[where_rows, :] = field[0:back, lanes(group * GROUP, 2 * GROUP)]
                    value = error[0:back, lanes(SIDE + group * GROUP, GROUP)]
                    value = jnp.where(inner_rows, value.astype(jnp.float32), 0.0)
                    bias_acc[which : which + 1, :] += jnp.sum(value, axis=0, keepdims=True)
                    tall_e[where_rows, 0:GROUP] = pltpu.roll(value, back - 1, 0).astype(
                        jnp.bfloat16
                    )
                    tall_e[where_rows, GROUP : 2 * GROUP] = value.astype(jnp.bfloat16)
                    tall_e[where_rows, 2 * GROUP :] = pltpu.roll(value, 1, 0).astype(
                        jnp.bfloat16
                    )

            each_group(groups, pile, chunk)
            grid_a[which] = lax.dot_general(
                tall_x[0 : groups * back, :],
                tall_e[0 : groups * back, :],
                (((0,), (0,)), ((), ())),
                preferred_element_type=jnp.float32,
            )

    for level in range(SECTIONS):

        @pl.when(section == level)
        def _():
            run_section(level)

    def folded(which, tap):
        dy, dx = tap // 3, tap % 3
        low, high = 0.0, 0.0
        for half in range(2):
            span_lanes = slice(GROUP * dy + SIDE * half, GROUP * dy + SIDE * half + SIDE)
            row = CH * (2 * half + dx + 1)
            low = low + grid_a[which, row : row + CH, span_lanes]
            high = high + grid_a[which, row + CH : row + 2 * CH, span_lanes]
        return low, high

    left = iota((CH, SIDE), 1) < CH
    blocks = []
    for pair in range(9):
        low_a, high_a = folded((2 * pair) // 9, (2 * pair) % 9)
        low_b, high_b = folded((2 * pair + 1) // 9, (2 * pair + 1) % 9)
        blocks.append(
            jnp.where(left, low_a + pltpu.roll(high_a, CH, 1), high_b + pltpu.roll(low_b, CH, 1))
        )
    sums = bias_acc[:, 0:SIDE] + bias_acc[:, SIDE:]
    sums = sums + pltpu.roll(sums, CH, 1)
    tail = jnp.where(iota((8, SIDE), 1) < CH, sums[0:1, :], sums[1:2, :])
    blocks.append(jnp.where(iota((8, SIDE), 0) == 0, tail, 0.0))
    blocks.append(jnp.zeros((PIECES * PIECE - 9 * CH - 8, SIDE), jnp.float32))
    packed[...] = jnp.concatenate(blocks, axis=0).reshape(PIECES, PIECE, SIDE)

    scale = 0.0
    for level, plan in enumerate(PLANS):
        factor = 1.0 / math.sqrt(strips * plan["rows"] * plan["cols"])
        scale = jnp.where(section == level, jnp.float32(factor), scale)

    def meanwhile():
        @pl.when(section == SECTIONS - 1)
        def _():
            finish_last()

    strip_sum(
        lambda a, b, c, d, peer: remote(a, b, c, d, (section, peer)),
        strip,
        scale,
        meanwhile,
        packed,
        *sum_refs,
    )
    sums_out[...] = sum_refs[7][...]

    x_down.wait_send()
    x_up.wait_send()

    @pl.when(section == 0)
    def _():
        c_down.wait_send()
        c_up.wait_send()

    for level in range(1, SECTIONS):

        @pl.when(section == level - 1)
        def _():
            for group in range(PLANS[level]["groups"]):
                hop(level, group, (coarser, strip)).wait_send()


def chain(x, cot, taps, bias):
    dma = pltpu.SemaphoreType.DMA
    half, full = jnp.bfloat16, jnp.float32
    padded = WIDE + 2 * SIDE
    in_vmem = pl.BlockSpec(memory_space=pltpu.VMEM)
    return pl.pallas_call(
        chain_body,
        out_shape=(
            jax.ShapeDtypeStruct((ROWS, COLS * CH), half),
            jax.ShapeDtypeStruct((PIECES, PIECE, SIDE), half),
        ),
        in_specs=[pl.BlockSpec(memory_space=pltpu.HBM)] * 4,
        out_specs=(in_vmem, in_vmem),
        scratch_shapes=[
            pltpu.VMEM((2 * BLOCK + ROWS, COLS * CH), half),
            pltpu.VMEM((2 * NARROW + ROWS, COLS * CH), half),
            pltpu.VMEM((4, 2 * GROUP, 3 * GROUP), half),
            pltpu.VMEM((TALL, padded), half),
            pltpu.VMEM((TALL, padded), half),
            pltpu.VMEM((TALL, padded), half),
            pltpu.VMEM((TALL, padded), half),
            pltpu.VMEM((TALL, WIDE), full),
            pltpu.VMEM((TALL, WIDE), full),
            pltpu.VMEM((TALL, WIDE), full),
            pltpu.VMEM((TALL, WIDE), half),
            pltpu.VMEM((TALL, WIDE), half),
            pltpu.VMEM((NEXT_TALL, WIDE), half),
            pltpu.VMEM((NEXT_TALL, NEXT_WIDE), half),
            pltpu.VMEM((NEXT_TALL, NEXT_WIDE), half),
            pltpu.VMEM((NEXT_WIDE // GROUP, 2 * GROUP, GROUP), half),
            pltpu.VMEM((DEEP, 2 * GROUP), half),
            pltpu.VMEM((DEEP, 3 * GROUP), half),
            pltpu.VMEM((2, 2 * GROUP, 3 * GROUP), full),
            pltpu.VMEM((2, GROUP), full),
            pltpu.VMEM((PIECES, PIECE, SIDE), full),
            pltpu.VMEM((2, 9, CH, CH), half),
            pltpu.VMEM((2, CH), full),
            dma((4,)),
            dma((2,)), dma((2,)), dma((2,)), dma((2,)),
            dma((NEXT_WIDE // GROUP,)), dma((NEXT_WIDE // GROUP,)),
            pltpu.VMEM((PIECES, PIECE, SIDE), half),
            pltpu.VMEM((RING, PIECE, SIDE), half),
            pltpu.VMEM((PIECE, SIDE), full),
            pltpu.VMEM((RING, PIECE, SIDE), half),
            pltpu.VMEM((RING - 1, PIECE, SIDE), half),
            pltpu.VMEM((PIECE, SIDE), half),
            pltpu.VMEM((RING, PIECE, SIDE), half),
            pltpu.VMEM((PIECES, PIECE, SIDE), half),
            dma((RING,)), dma((RING,)),
            dma((RING - 1,)), dma((RING - 1,)),
            dma((RING - 1,)), dma((RING - 1,)),
            dma((RING - 1,)), dma((RING - 1,)),
            dma((RING,)), dma((RING,)),
        ],
        compiler_params=pltpu.CompilerParams(
            collective_id=0, has_side_effects=True, vmem_limit_bytes=67043328
        ),
    )(x, cot, taps, bias)


def write_body(noise_in, sums_in, noise, kernel_out, bias_out, final):
    noise[...] = noise_in[...]
    final[...] = sums_in[...].astype(jnp.float32).reshape(PIECES * PIECE, SIDE)
    for pair in range(9):
        block = final[CH * pair : CH * pair + CH, :]
        kernel_out[2 * pair] = block[:, :CH]
        kernel_out[2 * pair + 1] = pltpu.roll(block, CH, 1)[:, :CH]
    sums = final[9 * CH : 9 * CH + 8, :]
    bias_out[0:1, :] = sums[0:1, :CH]
    bias_out[1:2, :] = pltpu.roll(sums, CH, 1)[0:1, :CH]


def write_out(noise, sums):
    in_vmem = pl.BlockSpec(memory_space=pltpu.VMEM)
    full = jnp.float32
    return pl.pallas_call(
        write_body,
        out_shape=(
            jax.ShapeDtypeStruct(noise.shape, noise.dtype),
            jax.ShapeDtypeStruct((18, CH, CH), full),
            jax.ShapeDtypeStruct((2, CH), full),
        ),
        in_specs=[in_vmem] * 2,
        out_specs=(in_vmem,) * 3,
        scratch_shapes=[pltpu.VMEM((PIECES * PIECE, SIDE), full)],
        compiler_params=pltpu.CompilerParams(vmem_limit_bytes=67043328),
    )(noise, sums)


def local(cotangent, activations, weights, biases):
    taps = weights.reshape(2, 9, CH, CH)
    noise, sums = chain(activations[0, 0], cotangent[0], taps, biases[0])
    noise, kernels, sums = write_out(noise, sums)
    return (
        noise[None, None],
        kernels.reshape(1, 2, 3, 3, CH, CH),
        sums[None],
    )


def solution(mesh):
    return jax.shard_map(
        local,
        mesh=mesh,
        in_specs=(
            P(None, "strip", None),
            P("section", None, "strip", None),
            P("section", None, None, None, None, None),
            P("section", None, None),
        ),
        out_specs=(
            P("section", None, "strip", None),
            P("section", None, None, None, None, None),
            P("section", None, None),
        ),
        check_vma=False,
    )
```
